32 devices in a mesh: elem: 16 (over z, x, core), section: 2 (over y).
Axes of the slice: x: 2, y: 2, z: 4, core: 2. Of those that a mesh axis runs over, the one named last changes fastest.
Arguments:
- u_start: float32 [512, 320], P('elem'), may hold values from -6 to 6
- inverses: float32 [512, 320, 320], P('elem'), may hold values from -1 to 2
- neighbours: int32 [512, 5], P('elem'), may hold values from 0 to 511, as said below
- partners: int32 [512], replicated, may hold values from 0 to 511, as said below
Outputs:
- section_states: float32 [4, 512, 320], P('section', 'elem')
The draws below stay inside these ranges and needn't reach their ends.
Inputs may be any that keep to these rules, and one draw needn't show every extreme that they name: `neighbours`: every entry names an element on the same device as the row's element, or on the device just before or after it along elem, cyclically. The partners of the 32 elements of device d along elem lie on devices d + 4 and d + 5, cyclically, 16 on each.
All inputs are finite; a program needn't handle non-finite values.
Results may differ from the reference program's by a relative error of at most 0.0001.
Values sent between devices are 32-bit elements; how exact they have to be, the bound alone decides.
A program may use at most 64 MiB of HBM per device.

```python
import math
import jax
import jax.numpy as jnp
from jax import lax

NODE1 = 4
UNK = 320
SECTIONS = 4
NEWTON = 2
E_DEV = 32
NE = 512


def draw_inverses(key, part):
    key_diag, key_off = jax.random.split(jax.random.fold_in(key, 11))
    diagonal_vals = jax.random.uniform(key_diag, (NE, UNK), jnp.float32, 0.6, 1.0)
    off_diag = jax.random.normal(key_off, (NE, UNK, UNK), jnp.float32) * (0.3 / UNK ** 0.5)
    return off_diag + diagonal_vals[:, :, None] * jnp.eye(UNK, dtype=jnp.float32)[None]


def draw_neighbours(key, part):
    devices = NE // E_DEV
    key_shift, key_local = jax.random.split(jax.random.fold_in(key, 23))
    shift_rows = jax.random.randint(key_shift, (NE, 5), -1, 2)
    owner_dev = (jnp.arange(NE, dtype=jnp.int32) // E_DEV)[:, None]
    target_dev = (owner_dev + shift_rows + devices) % devices
    local_rows = jax.random.randint(key_local, (NE, 5), 0, E_DEV)
    return (target_dev * E_DEV + local_rows).astype(jnp.int32)


def draw_partners(key, part):
    devices = NE // E_DEV
    rotation = devices // 4
    key_order, key_local = jax.random.split(jax.random.fold_in(key, 37))

    def slot_order(dev_key):
        return jax.random.permutation(dev_key, E_DEV)
    orders = jax.vmap(slot_order)(jax.random.split(key_order, devices))
    upper = (orders >= E_DEV // 2).astype(jnp.int32)
    device_ids = jnp.arange(devices, dtype=jnp.int32)[:, None]
    target_dev = (device_ids + rotation + upper) % devices
    local_rows = jax.random.randint(key_local, (devices, E_DEV), 0, E_DEV)
    return (target_dev * E_DEV + local_rows).reshape(NE).astype(jnp.int32)


def steps_of(key, shape, pieces, least, top_value):
    def one(axis_at, parts):
        draws = jax.random.uniform(jax.random.fold_in(jax.random.fold_in(key, 6), axis_at), (parts,), jnp.float32, least / len(pieces), top_value / len(pieces))
        return jnp.repeat(jnp.exp(draws), shape[axis_at] // parts).reshape((-1,) + (1,) * (len(shape) - axis_at - 1))

    factor_of = one(*pieces[0])
    for cut in pieces[1:]:
        factor_of = factor_of * one(*cut)
    return factor_of


def noise(rng, dims, scale, reach, cuts=(), kind=jnp.bfloat16):
    gain = steps_of(rng, dims, cuts, -0.22, 0.18) if cuts else 1.0
    result = jax.random.normal(rng, dims, jnp.float32) * scale * gain
    return jnp.minimum(jnp.maximum(result, -reach), reach).astype(kind)


def setup_inputs(seed: int = 0) -> dict:
    keys = jax.random.split(jax.random.key(seed), 5)
    u_start = noise(keys[0], (NE, UNK), 1.0, 6.0, ((0, 16),), jnp.float32)
    inverses = draw_inverses(jax.random.fold_in(keys[4], 71), 0)
    neighbours = draw_neighbours(jax.random.fold_in(keys[4], 71), 0)
    partners = draw_partners(jax.random.fold_in(keys[4], 71), 0)
    return dict(u_start=u_start, inverses=inverses, neighbours=neighbours, partners=partners)


time_step = 0.03
dissipation = 2.0
enthalpy_factor = 3.5
radau_nodes = [0.08858795951270394, 0.4094668644407347, 0.787659461760847, 1.0]

def lobatto():
    node_count = NODE1
    if node_count == 4:
        inner_value = 1.0 / math.sqrt(5.0)
        lobatto_nodes = [-1.0, -inner_value, inner_value, 1.0]
    else:
        lobatto_nodes = [-1.0, 1.0]
    products = []
    for row in range(node_count):
        value = 1.0
        for other in range(node_count):
            if other != row:
                value = value * (lobatto_nodes[row] - lobatto_nodes[other])
        products.append(value)
    derivative = []
    for row in range(node_count):
        entries = []
        for column in range(node_count):
            if row == column:
                total = 0.0
                for other in range(node_count):
                    if other != row:
                        total = total + 1.0 / (lobatto_nodes[row] - lobatto_nodes[other])
                entries.append(2.0 * total)
            else:
                entries.append(2.0 * (products[row] / products[column]) / (lobatto_nodes[row] - lobatto_nodes[column]))
        derivative.append(entries)
    return (jnp.asarray(derivative, jnp.float32), float(node_count * (node_count - 1) / 2.0))

def radau_table():
    section_total = SECTIONS
    butcher = []
    columns = []
    for column in range(section_total):
        coeffs = [1.0]
        scale = 1.0
        for other in range(section_total):
            if other != column:
                shifted = [0.0] + coeffs
                for position in range(len(coeffs)):
                    shifted[position] = shifted[position] - radau_nodes[other] * coeffs[position]
                coeffs = shifted
                scale = scale * (radau_nodes[column] - radau_nodes[other])
        integral = [0.0] + [coeffs[position] / (position + 1.0) / scale for position in range(len(coeffs))]
        columns.append(integral)
    for row in range(section_total):
        entries = []
        for column in range(section_total):
            value = 0.0
            for coefficient in reversed(columns[column]):
                value = value * radau_nodes[row] + coefficient
            entries.append(value)
        butcher.append(entries)
    return butcher

def flux(left_state, right_state, direction):
    density = 0.5 * (left_state[:, :, 0] + right_state[:, :, 0])
    velocity = [0.5 * (left_state[:, :, 1 + comp] + right_state[:, :, 1 + comp]) for comp in range(3)]
    pressure = 0.5 * (left_state[:, :, 4] + right_state[:, :, 4])
    kinetic = 0.0
    for comp in range(3):
        kinetic = kinetic + 0.5 * (left_state[:, :, 1 + comp] ** 2 + right_state[:, :, 1 + comp] ** 2)
    normal_speed = velocity[direction]
    mass_flux = density * normal_speed
    components = [mass_flux]
    for comp in range(3):
        momentum = mass_flux * velocity[comp]
        if comp == direction:
            momentum = momentum + pressure
        components.append(momentum)
    components.append(enthalpy_factor * pressure * normal_speed + 0.5 * mass_flux * kinetic)
    return jnp.stack(components, axis=2)

def face_list(node_grid):
    return [node_grid[:, :, :, 0], node_grid[:, :, :, -1], node_grid[:, :, :, :, 0], node_grid[:, :, :, :, -1], node_grid[:, :, :, :, :, 0], node_grid[:, :, :, :, :, -1]]

def lift(faces):
    shape = faces[0].shape[:3] + (NODE1, NODE1, NODE1)
    node_grid = jnp.zeros(shape, jnp.float32)
    node_grid = node_grid.at[:, :, :, 0].add(faces[0]).at[:, :, :, -1].add(faces[1])
    node_grid = node_grid.at[:, :, :, :, 0].add(faces[2]).at[:, :, :, :, -1].add(faces[3])
    node_grid = node_grid.at[:, :, :, :, :, 0].add(faces[4]).at[:, :, :, :, :, -1].add(faces[5])
    return node_grid

def traces(states):
    node_grid = states.reshape(states.shape[0], states.shape[1], 5, NODE1, NODE1, NODE1)
    return jnp.stack([face.reshape(states.shape[0], states.shape[1], -1) for face in face_list(node_grid)], axis=2)

def split_faces(neighbour_faces):
    return [neighbour_faces[:, :, face_index].reshape(neighbour_faces.shape[0], neighbour_faces.shape[1], 5, NODE1, NODE1) for face_index in range(6)]

def tendency(states, neighbour_faces, double_deriv, inv_weight):
    highest = lax.Precision.HIGHEST
    node_grid = states.reshape(states.shape[0], states.shape[1], 5, NODE1, NODE1, NODE1)
    flux_x = flux(node_grid[:, :, :, :, None, :, :], node_grid[:, :, :, None, :, :, :], 0)
    combined = jnp.einsum('il,seailjk->seaijk', double_deriv, flux_x, precision=highest)
    flux_y = flux(node_grid[:, :, :, :, :, None, :], node_grid[:, :, :, :, None, :, :], 1)
    combined = combined + jnp.einsum('jm,seaijmk->seaijk', double_deriv, flux_y, precision=highest)
    flux_z = flux(node_grid[:, :, :, :, :, :, None], node_grid[:, :, :, :, :, None, :], 2)
    combined = combined + jnp.einsum('kn,seaijkn->seaijk', double_deriv, flux_z, precision=highest)
    own_faces = face_list(node_grid)
    other_faces = split_faces(neighbour_faces)
    corrections = []
    for face_index in range(6):
        direction = face_index // 2
        normal_sign = 2.0 * (face_index % 2) - 1.0
        own_face = own_faces[face_index]
        other_face = other_faces[face_index]
        jump = flux(own_face, other_face, direction) - flux(own_face, own_face, direction)
        corrections.append(normal_sign * jump - 0.5 * dissipation * (other_face - own_face))
    combined = combined + inv_weight * lift(corrections)
    return (-2.0 * combined).reshape(states.shape)

def apply_inverse(inverses, vectors):
    return jnp.einsum('epq,seq->sep', inverses, vectors, precision=lax.Precision.HIGHEST)

def reference(u_start, inverses, neighbours, partners):
    double_deriv, inv_weight = lobatto()
    butcher = jnp.asarray(radau_table(), jnp.float32)
    coupling = time_step * jnp.diagonal(butcher) * dissipation * inv_weight
    opposite = [1, 0, 3, 2, 5]

    def gather_faces(face_traces):
        picked = [face_traces[:, neighbours[:, face_index], opposite[face_index]] for face_index in range(5)]
        picked.append(face_traces[:, partners, 4])
        return jnp.stack(picked, axis=2)
    states = jnp.broadcast_to(u_start[None], (SECTIONS,) + u_start.shape).astype(jnp.float32)
    for newton_round in range(NEWTON):
        tendencies = tendency(states, gather_faces(traces(states)), double_deriv, inv_weight)
        coupled = jnp.einsum('ij,jep->iep', butcher, tendencies, precision=lax.Precision.HIGHEST)
        residual = states - u_start[None] - time_step * coupled
        first_sweep = apply_inverse(inverses, -residual)
        lifted = lift(split_faces(gather_faces(traces(first_sweep)))).reshape(states.shape)
        second = apply_inverse(inverses, -residual + coupling[:, None, None] * lifted)
        states = states + second
    return states
```

```python
import functools
import math

import jax
import jax.numpy as jnp
from jax import lax
from jax.experimental import pallas as pl
from jax.experimental.pallas import tpu as pltpu
from jax.sharding import PartitionSpec as P

NODE1 = 4
SECTIONS = 4
NEWTON = 2


time_step = 0.03
dissipation = 2.0
enthalpy_factor = 3.5
radau_nodes = [0.08858795951270394, 0.4094668644407347, 0.787659461760847, 1.0]


def lobatto():
    node_count = NODE1
    inner_value = 1.0 / math.sqrt(5.0)
    lobatto_nodes = [-1.0, -inner_value, inner_value, 1.0]
    products = []
    for row in range(node_count):
        value = 1.0
        for other in range(node_count):
            if other != row:
                value = value * (lobatto_nodes[row] - lobatto_nodes[other])
        products.append(value)
    derivative = []
    for row in range(node_count):
        entries = []
        for column in range(node_count):
            if row == column:
                total = 0.0
                for other in range(node_count):
                    if other != row:
                        total = total + 1.0 / (lobatto_nodes[row] - lobatto_nodes[other])
                entries.append(2.0 * total)
            else:
                entries.append(
                    2.0
                    * (products[row] / products[column])
                    / (lobatto_nodes[row] - lobatto_nodes[column])
                )
        derivative.append(entries)
    return derivative, float(node_count * (node_count - 1) / 2.0)


def radau_table():
    section_total = SECTIONS
    butcher = []
    columns = []
    for column in range(section_total):
        coeffs = [1.0]
        scale = 1.0
        for other in range(section_total):
            if other != column:
                shifted = [0.0] + coeffs
                for position in range(len(coeffs)):
                    shifted[position] = shifted[position] - radau_nodes[other] * coeffs[position]
                coeffs = shifted
                scale = scale * (radau_nodes[column] - radau_nodes[other])
        integral = [0.0] + [
            coeffs[position] / (position + 1.0) / scale for position in range(len(coeffs))
        ]
        columns.append(integral)
    for row in range(section_total):
        entries = []
        for column in range(section_total):
            value = 0.0
            for coefficient in reversed(columns[column]):
                value = value * radau_nodes[row] + coefficient
            entries.append(value)
        butcher.append(entries)
    return butcher


FIELDS = 5
NODES = NODE1**3
FACE = NODE1**2
LANES = 128
GROUP = 8
ROWS = 64
MESH = pl.DeviceIdType.MESH


def strided(start, count):
    return pl.ds(start, count, stride=NODE1)


def to_k_order(src_ref, k_ref):
    for field in range(FIELDS):
        for k in range(NODE1):
            base = field * NODES
            k_ref[base + k * FACE : base + (k + 1) * FACE, :] = src_ref[strided(base + k, FACE), :]


def slab(src_ref, k_ref, direction, position):
    out = []
    for field in range(FIELDS):
        base = field * NODES
        if direction == 0:
            out.append(src_ref[base + position * FACE : base + (position + 1) * FACE, :])
        elif direction == 1:
            out.append(k_ref[strided(base + position, FACE), :])
        else:
            out.append(k_ref[base + position * FACE : base + (position + 1) * FACE, :])
    return out


def put_slabs(out_ref, k_ref, direction, slabs):
    for position in range(NODE1):
        for field in range(FIELDS):
            base = field * NODES
            rows = slice(base + position * FACE, base + (position + 1) * FACE)
            value = slabs[position][field]
            if direction == 0:
                out_ref[rows, :] = value
            elif direction == 1:
                k_ref[strided(base + position, FACE), :] = value
            else:
                value = k_ref[rows, :] + value
                there = strided(base + position, FACE)
                out_ref[there, :] = out_ref[there, :] + value


def speed2(state):
    return state[1] * state[1] + state[2] * state[2] + state[3] * state[3]


def two_point(a, ka, b, kb, direction):
    r = a[0] + b[0]
    v = [a[1 + c] + b[1 + c] for c in range(3)]
    p = a[4] + b[4]
    n = v[direction]
    m = (0.25 * r) * n
    half = 0.5 * m
    out = [m]
    for c in range(3):
        term = half * v[c]
        if c == direction:
            term = term + 0.5 * p
        out.append(term)
    out.append((0.25 * enthalpy_factor * p) * n + (0.5 * half) * (ka + kb))
    return out


def tendency(uc, uk, faces, out_ref, tk, scale):
    deriv, inv_weight = lobatto()
    for direction in range(3):
        states = [slab(uc, uk, direction, pos) for pos in range(NODE1)]
        speeds = [speed2(state) for state in states]
        sums = [None] * NODE1
        for a in range(NODE1):
            for b in range(a + 1, NODE1):
                f = two_point(states[a], speeds[a], states[b], speeds[b], direction)
                for at, other in ((a, b), (b, a)):
                    c = -2.0 * scale * deriv[at][other]
                    terms = [c * x for x in f]
                    sums[at] = terms if sums[at] is None else [x + y for x, y in zip(sums[at], terms)]
        for upper in range(2):
            pos = (NODE1 - 1) * upper
            sign = 2.0 * upper - 1.0
            other = faces(2 * direction + upper)
            f = two_point(states[pos], speeds[pos], other, speed2(other), direction)
            c = -2.0 * scale * inv_weight
            d = 0.5 * dissipation * c
            sums[pos] = [
                total + (c * sign) * x - d * (n - u)
                for total, x, n, u in zip(sums[pos], f, other, states[pos])
            ]
        put_slabs(out_ref, tk, direction, sums)


def lift(faces, out_ref, tk):
    zero = jnp.zeros((FACE, LANES), jnp.float32)
    for direction in range(3):
        slabs = [[zero] * FIELDS for _ in range(NODE1)]
        slabs[0] = faces(2 * direction)
        slabs[NODE1 - 1] = faces(2 * direction + 1)
        put_slabs(out_ref, tk, direction, slabs)


def kernel(
    devices, count, u_ref, nbr_ref, inv_ref, out_ref,
    a_ref, recv_ref, zrecv_ref, zsend_ref, pick_ref, near_ref,
    uc, uk, vc, wc, lc, tk, nc, nk, fc, gc, xr,
    a_sem, send_sem, recv_sem,
):
    rank = lax.axis_index("elem")
    part = lax.axis_index("section")
    parts = lax.axis_size("section")
    own_sections = SECTIONS // parts
    rotation = devices // 4
    unknowns = FIELDS * NODES
    butcher = radau_table()
    _, inv_weight = lobatto()
    groups = count // GROUP

    def at(offset):
        return lax.rem(rank + (offset + devices), devices)

    def load(g):
        block = pl.ds(g * GROUP, GROUP)
        return pltpu.make_async_copy(inv_ref.at[block], a_ref.at[block], a_sem.at[g])

    for g in range(groups):
        load(g).start()

    barrier = pltpu.get_barrier_semaphore()
    others = (1, -1, rotation, -rotation, rotation + 1, -rotation - 1)
    for offset in others:
        pl.semaphore_signal(barrier, inc=1, device_id={"elem": at(offset)}, device_id_type=MESH)
    pl.semaphore_wait(barrier, len(others))

    def copy(x, which):
        if which < 2:
            src = u_ref if x == 0 else recv_ref.at[x, pl.ds(2 * count, count)]
            dst = recv_ref.at[x, pl.ds(which * count, count)]
            target = at(1) if which == 0 else at(-1)
        else:
            src = zsend_ref.at[x]
            dst = zrecv_ref.at[x, pl.ds((which - 2) * count, count)]
            target = at(-rotation) if which == 2 else at(-rotation - 1)
        return pltpu.make_async_remote_copy(
            src_ref=src, dst_ref=dst, send_sem=send_sem.at[x, which],
            recv_sem=recv_sem.at[x, which], device_id={"elem": target}, device_id_type=MESH,
        )

    copy(0, 0).start()
    copy(0, 1).start()

    def lower_rows(col_ref):
        low = col_ref[strided(0, FIELDS * FACE), :]
        low = jnp.concatenate([low, jnp.zeros((LANES - FIELDS * FACE, LANES), jnp.float32)], axis=0)
        return low.T

    def send(x, col_ref, vectors):
        low = lower_rows(col_ref)
        for s in range(vectors):
            zsend_ref[x + s] = low[s * count : (s + 1) * count]
        for s in range(vectors):
            copy(x + s, 2).start()
            copy(x + s, 3).start()
        rows = col_ref[...].T
        for s in range(vectors):
            recv_ref[x + s, 2 * count : 3 * count] = rows[s * count : (s + 1) * count]
        for s in range(vectors):
            copy(x + s, 0).start()
            copy(x + s, 1).start()

    u_rows = u_ref[...]
    recv_ref[0, 2 * count : 3 * count] = u_rows
    uc[...] = jnp.concatenate([u_rows] * SECTIONS, axis=0).T
    zsend_ref[0] = lower_rows(uc)[:count]
    copy(0, 2).start()
    copy(0, 3).start()
    to_k_order(uc, uk)

    lane = lax.broadcasted_iota(jnp.int32, (1, LANES), 1)
    block = lane // count
    local = lane - block * count

    def ids(*offsets):
        out = jnp.full((1, LANES), -1, jnp.int32)
        for index, offset in enumerate(offsets):
            out = jnp.where(block == index, at(offset) * count + local, out)
        return out

    side_ids = ids(-1, 1, 0)
    sliding_ids = ids(rotation, rotation + 1)
    for face in range(6):
        match = nbr_ref[:, face : face + 1] == (side_ids if face < 5 else sliding_ids)
        match = jnp.where(match, 1.0, 0.0)
        pick_ref[face] = jnp.concatenate([match] * SECTIONS, axis=0).astype(jnp.bfloat16)

    def picked(face, values):
        high = values.astype(jnp.bfloat16)
        rest = values - high.astype(jnp.float32)
        middle = rest.astype(jnp.bfloat16)
        low = (rest - middle.astype(jnp.float32)).astype(jnp.bfloat16)
        split = jnp.concatenate([high, middle, low], axis=0)
        got = lax.dot_general(
            split, pick_ref[face], (((1,), (1,)), ((), ())), preferred_element_type=jnp.float32
        )
        n = values.shape[0]
        return (got[2 * n :] + got[n : 2 * n]) + got[:n]

    def receive(x, put):
        for which in range(4):
            copy(x, which).wait_recv()
        mine = recv_ref[x]
        nc[...] = jnp.concatenate([mine, mine[2 * count :]], axis=0).T
        to_k_order(nc, nk)
        for face in range(5):
            position = (NODE1 - 1) * (1 - face % 2)
            put(face, picked(face, jnp.concatenate(slab(nc, nk, face // 2, position), axis=0)))
        sliding = zrecv_ref[x]
        sliding = jnp.concatenate([sliding, sliding], axis=0).T
        put(5, picked(5, sliding[: FIELDS * FACE]))

    def keep(slot):
        def put(face, value):
            near_ref[slot, face] = value
        return put

    def near(slot):
        def faces(face):
            return [near_ref[slot, face, f * FACE : (f + 1) * FACE, :] for f in range(FIELDS)]
        return faces

    def per_lane(value_of):
        out = jnp.zeros((1, LANES), jnp.float32)
        for group in range(SECTIONS):
            value = jnp.float32(value_of(0, group))
            for other in range(1, parts):
                value = jnp.where(part == other, jnp.float32(value_of(other, group)), value)
            out = jnp.where(block == group, value, out)
        return out

    def matvec(dst, vectors, first):
        dst[...] = jnp.zeros_like(dst)

        @pl.loop(0, groups)
        def _(g):
            if first:
                load(g).wait()
            xs = [
                xr[pl.ds(pl.multiple_of(s * count + g * GROUP, GROUP), GROUP), :]
                for s in range(vectors)
            ]

            @pl.loop(0, unknowns // ROWS)
            def _(c):
                rows = pl.ds(pl.multiple_of(c * ROWS, ROWS), ROWS)
                acc = dst[rows, :]
                for k in range(GROUP):
                    e = g * GROUP + k
                    a = a_ref[e, rows, :]
                    for s in range(vectors):
                        total = jnp.sum(a * xs[s][k : k + 1, :], axis=1, keepdims=True)
                        where = local == e if vectors == 1 else lane == s * count + e
                        acc = jnp.where(where, total, acc)
                dst[rows, :] = acc

    receive(0, keep(0))
    tendency(uc, uk, near(0), lc, tk, 1.0)
    xr[...] = lc[...].T
    matvec(vc, 1, True)
    send(1, vc, 1)
    receive(1, keep(1))
    lift(near(1), lc, tk)
    xr[...] = lc[...].T
    matvec(wc, 1, False)
    send(2, wc, 1)

    def alpha(i):
        return time_step * sum(butcher[i])

    def coupling(i):
        return time_step * butcher[i][i] * dissipation * inv_weight

    def own(p, group):
        return p * own_sections + group % own_sections

    alphas = per_lane(lambda p, s: alpha(s))
    betas = per_lane(lambda p, s: alpha(s) * coupling(s))
    gc[...] = uc[...] + alphas * vc[...] + betas * wc[...]
    to_k_order(gc, uk)

    def add(face, value):
        near_ref[0, face] = near_ref[0, face] + alphas * near_ref[1, face] + betas * value

    receive(2, add)
    tendency(gc, uk, near(0), lc, tk, time_step)

    own_alphas = per_lane(lambda p, g: alpha(own(p, g)))
    own_betas = per_lane(lambda p, g: alpha(own(p, g)) * coupling(own(p, g)))
    own_couplings = per_lane(lambda p, g: coupling(own(p, g)))
    step = own_alphas * vc[...] + own_betas * wc[...]
    tend = lc[...]
    total = -step
    for shift in range(SECTIONS):
        moved = tend if shift == 0 else pltpu.roll(tend, shift * count, 1)
        weights = per_lane(lambda p, g: butcher[own(p, g)][(g - shift) % SECTIONS])
        total = total + weights * moved
    gc[...] = uc[...] + step
    xr[...] = total.T
    matvec(fc, own_sections, False)
    send(3, fc, own_sections)
    receive(3, keep(0))
    for s in range(1, own_sections):
        def merge(face, value, s=s):
            near_ref[0, face] = jnp.where(block == s, value, near_ref[0, face])
        receive(3 + s, merge)
    lift(near(0), lc, tk)
    xr[...] = (own_couplings * lc[...]).T
    matvec(wc, own_sections, False)
    rows = (gc[...] + fc[...] + wc[...]).T
    for s in range(own_sections):
        out_ref[s] = rows[s * count : (s + 1) * count]
    for x in range(3 + own_sections):
        for which in range(4):
            copy(x, which).wait_send()


def on_device(u_start, inverses, neighbours, partners):
    count, unknowns = u_start.shape
    devices = lax.axis_size("elem")
    own_sections = SECTIONS // lax.axis_size("section")
    mine = lax.dynamic_slice_in_dim(partners, lax.axis_index("elem") * count, count, 0)
    six = jnp.concatenate([neighbours, mine[:, None]], axis=1)
    exchanges = 3 + own_sections
    column = pltpu.VMEM((unknowns, LANES), jnp.float32)
    vmem = pl.BlockSpec(memory_space=pltpu.VMEM)
    return pl.pallas_call(
        functools.partial(kernel, devices, count),
        out_shape=jax.ShapeDtypeStruct((own_sections, count, unknowns), jnp.float32),
        in_specs=[vmem, vmem, pl.BlockSpec(memory_space=pl.ANY)],
        out_specs=vmem,
        scratch_shapes=[
            pltpu.VMEM((count, unknowns, unknowns), jnp.float32),
            pltpu.VMEM((exchanges, 3 * count, unknowns), jnp.float32),
            pltpu.VMEM((exchanges, 2 * count, LANES), jnp.float32),
            pltpu.VMEM((exchanges, count, LANES), jnp.float32),
            pltpu.VMEM((6, LANES, LANES), jnp.bfloat16),
            pltpu.VMEM((2, 6, FIELDS * FACE, LANES), jnp.float32),
        ]
        + [column] * 10
        + [
            pltpu.VMEM((LANES, unknowns), jnp.float32),
            pltpu.SemaphoreType.DMA((count // GROUP,)),
            pltpu.SemaphoreType.DMA((exchanges, 4)),
            pltpu.SemaphoreType.DMA((exchanges, 4)),
        ],
        compiler_params=pltpu.CompilerParams(
            collective_id=0, has_side_effects=True, vmem_limit_bytes=60 * 1024 * 1024
        ),
    )(u_start, six, inverses)


def solution(mesh):
    placed = (P("elem", None), P("elem", None, None), P("elem", None), P())
    return jax.shard_map(
        on_device, mesh=mesh, in_specs=placed, out_specs=P("section", "elem", None), check_vma=False
    )
```

```python
import functools
import math

import jax
import jax.numpy as jnp
from jax import lax
from jax.experimental import pallas as pl
from jax.experimental.pallas import tpu as pltpu
from jax.sharding import PartitionSpec as P

NODE1 = 4
SECTIONS = 4
NEWTON = 2


time_step = 0.03
dissipation = 2.0
enthalpy_factor = 3.5
radau_nodes = [0.08858795951270394, 0.4094668644407347, 0.787659461760847, 1.0]


def lobatto():
    node_count = NODE1
    inner_value = 1.0 / math.sqrt(5.0)
    lobatto_nodes = [-1.0, -inner_value, inner_value, 1.0]
    products = []
    for row in range(node_count):
        value = 1.0
        for other in range(node_count):
            if other != row:
                value = value * (lobatto_nodes[row] - lobatto_nodes[other])
        products.append(value)
    derivative = []
    for row in range(node_count):
        entries = []
        for column in range(node_count):
            if row == column:
                total = 0.0
                for other in range(node_count):
                    if other != row:
                        total = total + 1.0 / (lobatto_nodes[row] - lobatto_nodes[other])
                entries.append(2.0 * total)
            else:
                entries.append(
                    2.0
                    * (products[row] / products[column])
                    / (lobatto_nodes[row] - lobatto_nodes[column])
                )
        derivative.append(entries)
    return derivative, float(node_count * (node_count - 1) / 2.0)


def radau_table():
    section_total = SECTIONS
    butcher = []
    columns = []
    for column in range(section_total):
        coeffs = [1.0]
        scale = 1.0
        for other in range(section_total):
            if other != column:
                shifted = [0.0] + coeffs
                for position in range(len(coeffs)):
                    shifted[position] = shifted[position] - radau_nodes[other] * coeffs[position]
                coeffs = shifted
                scale = scale * (radau_nodes[column] - radau_nodes[other])
        integral = [0.0] + [
            coeffs[position] / (position + 1.0) / scale for position in range(len(coeffs))
        ]
        columns.append(integral)
    for row in range(section_total):
        entries = []
        for column in range(section_total):
            value = 0.0
            for coefficient in reversed(columns[column]):
                value = value * radau_nodes[row] + coefficient
            entries.append(value)
        butcher.append(entries)
    return butcher


FIELDS = 5
NODES = NODE1**3
FACE = NODE1**2
LANES = 128
GROUP = 8
ROWS = 64
MESH = pl.DeviceIdType.MESH


def strided(start, count):
    return pl.ds(start, count, stride=NODE1)


def to_k_order(src_ref, k_ref):
    for field in range(FIELDS):
        for k in range(NODE1):
            base = field * NODES
            k_ref[base + k * FACE : base + (k + 1) * FACE, :] = src_ref[strided(base + k, FACE), :]


def slab(src_ref, k_ref, direction, position):
    out = []
    for field in range(FIELDS):
        base = field * NODES
        if direction == 0:
            out.append(src_ref[base + position * FACE : base + (position + 1) * FACE, :])
        elif direction == 1:
            out.append(k_ref[strided(base + position, FACE), :])
        else:
            out.append(k_ref[base + position * FACE : base + (position + 1) * FACE, :])
    return out


def put_slabs(out_ref, k_ref, direction, slabs):
    for position in range(NODE1):
        for field in range(FIELDS):
            base = field * NODES
            rows = slice(base + position * FACE, base + (position + 1) * FACE)
            value = slabs[position][field]
            if direction == 0:
                out_ref[rows, :] = value
            elif direction == 1:
                k_ref[strided(base + position, FACE), :] = value
            else:
                value = k_ref[rows, :] + value
                there = strided(base + position, FACE)
                out_ref[there, :] = out_ref[there, :] + value


def speed2(state):
    return state[1] * state[1] + state[2] * state[2] + state[3] * state[3]


def two_point(a, ka, b, kb, direction):
    r = a[0] + b[0]
    v = [a[1 + c] + b[1 + c] for c in range(3)]
    p = a[4] + b[4]
    n = v[direction]
    m = (0.25 * r) * n
    half = 0.5 * m
    out = [m]
    for c in range(3):
        term = half * v[c]
        if c == direction:
            term = term + 0.5 * p
        out.append(term)
    out.append((0.25 * enthalpy_factor * p) * n + (0.5 * half) * (ka + kb))
    return out


def volume(uc, uk, out_ref, tk, scale):
    deriv, _ = lobatto()
    for direction in range(3):
        states = [slab(uc, uk, direction, pos) for pos in range(NODE1)]
        speeds = [speed2(state) for state in states]
        sums = [None] * NODE1
        for a in range(NODE1):
            for b in range(a + 1, NODE1):
                f = two_point(states[a], speeds[a], states[b], speeds[b], direction)
                for at, other in ((a, b), (b, a)):
                    c = -2.0 * scale * deriv[at][other]
                    terms = [c * x for x in f]
                    sums[at] = terms if sums[at] is None else [x + y for x, y in zip(sums[at], terms)]
        put_slabs(out_ref, tk, direction, sums)


def surface(uc, uk, faces, out_ref, tk, scale):
    _, inv_weight = lobatto()

    def terms(face):
        direction, upper = face // 2, face % 2
        own = slab(uc, uk, direction, (NODE1 - 1) * upper)
        other = faces(face)
        f = two_point(own, speed2(own), other, speed2(other), direction)
        c = -2.0 * scale * inv_weight
        d = 0.5 * dissipation * c
        sign = 2.0 * upper - 1.0
        return [(c * sign) * x - d * (n - u) for x, n, u in zip(f, other, own)]

    add_faces(terms, out_ref, tk)


def add_faces(terms, out_ref, tk):
    zero = jnp.zeros((FACE, LANES), jnp.float32)
    for face in range(6):
        direction, position = face // 2, (NODE1 - 1) * (face % 2)
        values = terms(face)
        for field in range(FIELDS):
            base = field * NODES
            rows = slice(base + position * FACE, base + (position + 1) * FACE)
            there = strided(base + position, FACE)
            if direction == 0:
                out_ref[rows, :] = out_ref[rows, :] + values[field]
            elif direction == 1:
                tk[there, :] = values[field]
                if face == 3:
                    for inner in range(1, NODE1 - 1):
                        tk[strided(base + inner, FACE), :] = zero
            else:
                tk[rows, :] = tk[rows, :] + values[field]
    for field in range(FIELDS):
        base = field * NODES
        for position in range(NODE1):
            rows = slice(base + position * FACE, base + (position + 1) * FACE)
            there = strided(base + position, FACE)
            out_ref[there, :] = out_ref[there, :] + tk[rows, :]


def lift(faces, out_ref, tk):
    zero = jnp.zeros((FACE, LANES), jnp.float32)
    for direction in range(3):
        slabs = [[zero] * FIELDS for _ in range(NODE1)]
        slabs[0] = faces(2 * direction)
        slabs[NODE1 - 1] = faces(2 * direction + 1)
        put_slabs(out_ref, tk, direction, slabs)


def kernel(
    devices, count, u_ref, nbr_ref, partner_ref, inv_ref, out_ref,
    a_ref, recv_ref, zrecv_ref, zsend_ref, pick_ref, near_ref,
    uc, uk, vc, wc, lc, tk, nc, nk, fc, gc, xr,
    a_sem, send_sem, recv_sem,
):
    rank = lax.axis_index("elem")
    part = lax.axis_index("section")
    parts = lax.axis_size("section")
    own_sections = SECTIONS // parts
    rotation = devices // 4
    unknowns = FIELDS * NODES
    butcher = radau_table()
    _, inv_weight = lobatto()
    groups = count // GROUP

    def at(offset):
        return lax.rem(rank + (offset + devices), devices)

    def load(g):
        block = pl.ds(g * GROUP, GROUP)
        return pltpu.make_async_copy(inv_ref.at[block], a_ref.at[block], a_sem.at[g])

    for g in range(groups):
        load(g).start()

    barrier = pltpu.get_barrier_semaphore()
    others = (1, -1, rotation, -rotation, rotation + 1, -rotation - 1)
    for offset in others:
        pl.semaphore_signal(barrier, inc=1, device_id={"elem": at(offset)}, device_id_type=MESH)

    def copy(x, which):
        if which < 2:
            src = u_ref if x == 0 else recv_ref.at[x, pl.ds(2 * count, count)]
            dst = recv_ref.at[x, pl.ds(which * count, count)]
            target = at(1) if which == 0 else at(-1)
        else:
            src = zsend_ref.at[x]
            dst = zrecv_ref.at[x, pl.ds((which - 2) * count, count)]
            target = at(-rotation) if which == 2 else at(-rotation - 1)
        return pltpu.make_async_remote_copy(
            src_ref=src, dst_ref=dst, send_sem=send_sem.at[x, which],
            recv_sem=recv_sem.at[x, which], device_id={"elem": target}, device_id_type=MESH,
        )

    def lower_rows(col_ref):
        low = col_ref[strided(0, FIELDS * FACE), :]
        low = jnp.concatenate([low, jnp.zeros((LANES - FIELDS * FACE, LANES), jnp.float32)], axis=0)
        return low.T

    def send(x, col_ref, vectors):
        low = lower_rows(col_ref)
        for s in range(vectors):
            zsend_ref[x + s] = low[s * count : (s + 1) * count]
        for s in range(vectors):
            copy(x + s, 3).start()
            copy(x + s, 2).start()
        rows = col_ref[...].T
        for s in range(vectors):
            recv_ref[x + s, 2 * count : 3 * count] = rows[s * count : (s + 1) * count]
        for s in range(vectors):
            copy(x + s, 0).start()
            copy(x + s, 1).start()

    u_rows = u_ref[...]
    uc[...] = jnp.concatenate([u_rows] * SECTIONS, axis=0).T
    zsend_ref[0] = lower_rows(uc)[:count]
    recv_ref[0, 2 * count : 3 * count] = u_rows
    pl.semaphore_wait(barrier, len(others))
    copy(0, 3).start()
    copy(0, 2).start()
    copy(0, 0).start()
    copy(0, 1).start()
    to_k_order(uc, uk)
    volume(uc, uk, lc, tk, 1.0)

    lane = lax.broadcasted_iota(jnp.int32, (1, LANES), 1)
    block = lane // count
    local = lane - block * count
    row = lax.broadcasted_iota(jnp.int32, (LANES, 1), 0)

    def ids(*offsets):
        out = jnp.full((LANES, 1), -1, jnp.int32)
        for index, offset in enumerate(offsets):
            inside = (row >= index * count) & (row < (index + 1) * count)
            out = jnp.where(inside, at(offset) * count + row - index * count, out)
        return out

    side_ids = ids(-1, 1, 0)
    sliding_ids = ids(rotation, rotation + 1)
    per_row = LANES // count
    listed = partner_ref[pl.ds(rank // per_row, 1), :]
    partner = jnp.zeros((1, LANES), jnp.int32)
    for index in range(per_row):
        part_row = jnp.concatenate([listed[:, index * count : (index + 1) * count]] * SECTIONS, axis=1)
        partner = jnp.where(rank % per_row == index, part_row, partner)
    for face in range(6):
        if face < 5:
            wanted = jnp.concatenate([nbr_ref[face : face + 1, :]] * SECTIONS, axis=1)
            match = side_ids == wanted
        else:
            match = sliding_ids == partner
        pick_ref[face] = jnp.where(match, 1.0, 0.0).astype(jnp.bfloat16)

    def picked(face, values):
        high = values.astype(jnp.bfloat16)
        rest = values - high.astype(jnp.float32)
        middle = rest.astype(jnp.bfloat16)
        low = (rest - middle.astype(jnp.float32)).astype(jnp.bfloat16)
        split = jnp.concatenate([high, middle, low], axis=0)
        got = lax.dot_general(
            split, pick_ref[face], (((1,), (0,)), ((), ())), preferred_element_type=jnp.float32
        )
        n = values.shape[0]
        return (got[2 * n :] + got[n : 2 * n]) + got[:n]

    def receive(x, put):
        for which in range(4):
            copy(x, which).wait_recv()
        mine = recv_ref[x]
        nc[...] = jnp.concatenate([mine, mine[2 * count :]], axis=0).T
        to_k_order(nc, nk)
        for face in range(5):
            position = (NODE1 - 1) * (1 - face % 2)
            put(face, picked(face, jnp.concatenate(slab(nc, nk, face // 2, position), axis=0)))
        sliding = zrecv_ref[x]
        sliding = jnp.concatenate([sliding, sliding], axis=0).T
        put(5, picked(5, sliding[: FIELDS * FACE]))

    def keep(slot):
        def put(face, value):
            near_ref[slot, face] = value
        return put

    def near(slot):
        def faces(face):
            return [near_ref[slot, face, f * FACE : (f + 1) * FACE, :] for f in range(FIELDS)]
        return faces

    def per_lane(value_of):
        out = jnp.zeros((1, LANES), jnp.float32)
        for group in range(SECTIONS):
            value = jnp.float32(value_of(0, group))
            for other in range(1, parts):
                value = jnp.where(part == other, jnp.float32(value_of(other, group)), value)
            out = jnp.where(block == group, value, out)
        return out

    def matvec(dst, vectors, first):
        dst[...] = jnp.zeros_like(dst)

        @pl.loop(0, groups)
        def _(g):
            if first:
                load(g).wait()
            xs = [
                xr[pl.ds(pl.multiple_of(s * count + g * GROUP, GROUP), GROUP), :]
                for s in range(vectors)
            ]

            for c in range(unknowns // ROWS):
                rows = slice(c * ROWS, (c + 1) * ROWS)
                acc = dst[rows, :]
                for k in range(GROUP):
                    e = g * GROUP + k
                    a = a_ref[e, rows, :]
                    for s in range(vectors):
                        total = jnp.sum(a * xs[s][k : k + 1, :], axis=1, keepdims=True)
                        where = local == e if vectors == 1 else lane == s * count + e
                        acc = jnp.where(where, total, acc)
                dst[rows, :] = acc

    receive(0, keep(0))
    surface(uc, uk, near(0), lc, tk, 1.0)
    xr[...] = lc[...].T
    matvec(vc, 1, True)
    send(1, vc, 1)
    receive(1, keep(1))
    lift(near(1), lc, tk)
    xr[...] = lc[...].T
    matvec(wc, 1, False)
    send(2, wc, 1)

    def alpha(i):
        return time_step * sum(butcher[i])

    def coupling(i):
        return time_step * butcher[i][i] * dissipation * inv_weight

    def own(p, group):
        return p * own_sections + group % own_sections

    alphas = per_lane(lambda p, s: alpha(s))
    betas = per_lane(lambda p, s: alpha(s) * coupling(s))
    gc[...] = uc[...] + alphas * vc[...] + betas * wc[...]
    to_k_order(gc, uk)

    def add(face, value):
        near_ref[0, face] = near_ref[0, face] + alphas * near_ref[1, face] + betas * value

    volume(gc, uk, lc, tk, time_step)
    receive(2, add)
    surface(gc, uk, near(0), lc, tk, time_step)

    own_alphas = per_lane(lambda p, g: alpha(own(p, g)))
    own_betas = per_lane(lambda p, g: alpha(own(p, g)) * coupling(own(p, g)))
    own_couplings = per_lane(lambda p, g: coupling(own(p, g)))
    step = own_alphas * vc[...] + own_betas * wc[...]
    tend = lc[...]
    total = -step
    for shift in range(SECTIONS):
        moved = tend if shift == 0 else pltpu.roll(tend, shift * count, 1)
        weights = per_lane(lambda p, g: butcher[own(p, g)][(g - shift) % SECTIONS])
        total = total + weights * moved
    gc[...] = step
    xr[...] = total.T
    matvec(fc, own_sections, False)
    send(3, fc, own_sections)
    receive(3, keep(0))
    for s in range(1, own_sections):
        def merge(face, value, s=s):
            near_ref[0, face] = jnp.where(block == s, value, near_ref[0, face])
        receive(3 + s, merge)
    lift(near(0), lc, tk)
    xr[...] = (own_couplings * lc[...]).T
    matvec(wc, own_sections, False)
    rows = (gc[...] + fc[...] + wc[...]).T
    for s in range(own_sections):
        out_ref[s] = rows[s * count : (s + 1) * count]
    for x in range(3 + own_sections):
        for which in range(4):
            copy(x, which).wait_send()


def on_device(u_start, inverses, neighbours, partners):
    count, unknowns = u_start.shape
    devices = lax.axis_size("elem")
    own_sections = SECTIONS // lax.axis_size("section")
    listed = partners.reshape(-1, LANES)
    exchanges = 3 + own_sections
    column = pltpu.VMEM((unknowns, LANES), jnp.float32)
    vmem = pl.BlockSpec(memory_space=pltpu.VMEM)
    change = pl.pallas_call(
        functools.partial(kernel, devices, count),
        out_shape=jax.ShapeDtypeStruct((own_sections, count, unknowns), jnp.float32),
        in_specs=[vmem, vmem, vmem, pl.BlockSpec(memory_space=pl.ANY)],
        out_specs=vmem,
        scratch_shapes=[
            pltpu.VMEM((count, unknowns, unknowns), jnp.float32),
            pltpu.VMEM((exchanges, 3 * count, unknowns), jnp.float32),
            pltpu.VMEM((exchanges, 2 * count, LANES), jnp.float32),
            pltpu.VMEM((exchanges, count, LANES), jnp.float32),
            pltpu.VMEM((6, LANES, LANES), jnp.bfloat16),
            pltpu.VMEM((2, 6, FIELDS * FACE, LANES), jnp.float32),
        ]
        + [column] * 10
        + [
            pltpu.VMEM((LANES, unknowns), jnp.float32),
            pltpu.SemaphoreType.DMA((count // GROUP,)),
            pltpu.SemaphoreType.DMA((exchanges, 4)),
            pltpu.SemaphoreType.DMA((exchanges, 4)),
        ],
        compiler_params=pltpu.CompilerParams(
            collective_id=0, has_side_effects=True, vmem_limit_bytes=60 * 1024 * 1024
        ),
    )(u_start, neighbours.T, listed, inverses)
    return u_start[None] + change


def solution(mesh):
    placed = (P("elem", None), P("elem", None, None), P("elem", None), P())
    return jax.shard_map(
        on_device, mesh=mesh, in_specs=placed, out_specs=P("section", "elem", None), check_vma=False
    )
```

```python
import functools
import math

import jax
import jax.numpy as jnp
from jax import lax
from jax.experimental import pallas as pl
from jax.experimental.pallas import tpu as pltpu
from jax.sharding import PartitionSpec as P

NODE1 = 4
SECTIONS = 4
NEWTON = 2


time_step = 0.03
dissipation = 2.0
enthalpy_factor = 3.5
radau_nodes = [0.08858795951270394, 0.4094668644407347, 0.787659461760847, 1.0]


def lobatto():
    node_count = NODE1
    inner_value = 1.0 / math.sqrt(5.0)
    lobatto_nodes = [-1.0, -inner_value, inner_value, 1.0]
    products = []
    for row in range(node_count):
        value = 1.0
        for other in range(node_count):
            if other != row:
                value = value * (lobatto_nodes[row] - lobatto_nodes[other])
        products.append(value)
    derivative = []
    for row in range(node_count):
        entries = []
        for column in range(node_count):
            if row == column:
                total = 0.0
                for other in range(node_count):
                    if other != row:
                        total = total + 1.0 / (lobatto_nodes[row] - lobatto_nodes[other])
                entries.append(2.0 * total)
            else:
                entries.append(
                    2.0
                    * (products[row] / products[column])
                    / (lobatto_nodes[row] - lobatto_nodes[column])
                )
        derivative.append(entries)
    return derivative, float(node_count * (node_count - 1) / 2.0)


def radau_table():
    section_total = SECTIONS
    butcher = []
    columns = []
    for column in range(section_total):
        coeffs = [1.0]
        scale = 1.0
        for other in range(section_total):
            if other != column:
                shifted = [0.0] + coeffs
                for position in range(len(coeffs)):
                    shifted[position] = shifted[position] - radau_nodes[other] * coeffs[position]
                coeffs = shifted
                scale = scale * (radau_nodes[column] - radau_nodes[other])
        integral = [0.0] + [
            coeffs[position] / (position + 1.0) / scale for position in range(len(coeffs))
        ]
        columns.append(integral)
    for row in range(section_total):
        entries = []
        for column in range(section_total):
            value = 0.0
            for coefficient in reversed(columns[column]):
                value = value * radau_nodes[row] + coefficient
            entries.append(value)
        butcher.append(entries)
    return butcher


FIELDS = 5
NODES = NODE1**3
FACE = NODE1**2
LANES = 128
GROUP = 8
ROWS = 64
MESH = pl.DeviceIdType.MESH


def strided(start, count):
    return pl.ds(start, count, stride=NODE1)


def to_k_order(src_ref, k_ref):
    for field in range(FIELDS):
        for k in range(NODE1):
            base = field * NODES
            k_ref[base + k * FACE : base + (k + 1) * FACE, :] = src_ref[strided(base + k, FACE), :]


def slab(src_ref, k_ref, direction, position):
    out = []
    for field in range(FIELDS):
        base = field * NODES
        if direction == 0:
            out.append(src_ref[base + position * FACE : base + (position + 1) * FACE, :])
        elif direction == 1:
            out.append(k_ref[strided(base + position, FACE), :])
        else:
            out.append(k_ref[base + position * FACE : base + (position + 1) * FACE, :])
    return out


def put_slabs(out_ref, k_ref, direction, slabs):
    for position in range(NODE1):
        for field in range(FIELDS):
            base = field * NODES
            rows = slice(base + position * FACE, base + (position + 1) * FACE)
            value = slabs[position][field]
            if direction == 0:
                out_ref[rows, :] = value
            elif direction == 1:
                k_ref[strided(base + position, FACE), :] = value
            else:
                value = k_ref[rows, :] + value
                there = strided(base + position, FACE)
                out_ref[there, :] = out_ref[there, :] + value


def speed2(state):
    return state[1] * state[1] + state[2] * state[2] + state[3] * state[3]


def two_point(a, ka, b, kb, direction):
    r = a[0] + b[0]
    v = [a[1 + c] + b[1 + c] for c in range(3)]
    p = a[4] + b[4]
    n = v[direction]
    m = (0.25 * r) * n
    half = 0.5 * m
    out = [m]
    for c in range(3):
        term = half * v[c]
        if c == direction:
            term = term + 0.5 * p
        out.append(term)
    out.append((0.25 * enthalpy_factor * p) * n + (0.5 * half) * (ka + kb))
    return out


def volume(uc, uk, out_ref, tk, scale):
    deriv, _ = lobatto()
    for direction in range(3):
        states = [slab(uc, uk, direction, pos) for pos in range(NODE1)]
        speeds = [speed2(state) for state in states]
        sums = [None] * NODE1
        for a in range(NODE1):
            for b in range(a + 1, NODE1):
                f = two_point(states[a], speeds[a], states[b], speeds[b], direction)
                for at, other in ((a, b), (b, a)):
                    c = -2.0 * scale * deriv[at][other]
                    terms = [c * x for x in f]
                    sums[at] = terms if sums[at] is None else [x + y for x, y in zip(sums[at], terms)]
        put_slabs(out_ref, tk, direction, sums)


def surface(uc, uk, faces, out_ref, tk, scale):
    _, inv_weight = lobatto()

    def terms(face):
        direction, upper = face // 2, face % 2
        own = slab(uc, uk, direction, (NODE1 - 1) * upper)
        other = faces(face)
        f = two_point(own, speed2(own), other, speed2(other), direction)
        c = -2.0 * scale * inv_weight
        d = 0.5 * dissipation * c
        sign = 2.0 * upper - 1.0
        return [(c * sign) * x - d * (n - u) for x, n, u in zip(f, other, own)]

    add_faces(terms, out_ref, tk)


def add_faces(terms, out_ref, tk):
    zero = jnp.zeros((FACE, LANES), jnp.float32)
    for face in range(6):
        direction, position = face // 2, (NODE1 - 1) * (face % 2)
        values = terms(face)
        for field in range(FIELDS):
            base = field * NODES
            rows = slice(base + position * FACE, base + (position + 1) * FACE)
            there = strided(base + position, FACE)
            if direction == 0:
                out_ref[rows, :] = out_ref[rows, :] + values[field]
            elif direction == 1:
                tk[there, :] = values[field]
                if face == 3:
                    for inner in range(1, NODE1 - 1):
                        tk[strided(base + inner, FACE), :] = zero
            else:
                tk[rows, :] = tk[rows, :] + values[field]
    for field in range(FIELDS):
        base = field * NODES
        for position in range(NODE1):
            rows = slice(base + position * FACE, base + (position + 1) * FACE)
            there = strided(base + position, FACE)
            out_ref[there, :] = out_ref[there, :] + tk[rows, :]


def lift(faces, out_ref, tk):
    zero = jnp.zeros((FACE, LANES), jnp.float32)
    for direction in range(3):
        slabs = [[zero] * FIELDS for _ in range(NODE1)]
        slabs[0] = faces(2 * direction)
        slabs[NODE1 - 1] = faces(2 * direction + 1)
        put_slabs(out_ref, tk, direction, slabs)


def kernel(
    devices, count, u_ref, nbr_ref, partner_ref, inv_ref, out_ref,
    a_ref, recv_ref, zrecv_ref, zsend_ref, pick_ref, near_ref,
    uc, uk, vc, wc, lc, tk, nc, nk, fc, gc, grp, xr,
    a_sem, send_sem, recv_sem,
):
    rank = lax.axis_index("elem")
    part = lax.axis_index("section")
    parts = lax.axis_size("section")
    own_sections = SECTIONS // parts
    rotation = devices // 4
    unknowns = FIELDS * NODES
    butcher = radau_table()
    _, inv_weight = lobatto()
    groups = count // GROUP

    def at(offset):
        return lax.rem(rank + (offset + devices), devices)

    def load(g):
        block = pl.ds(g * GROUP, GROUP)
        return pltpu.make_async_copy(inv_ref.at[block], a_ref.at[block], a_sem.at[g])

    for g in range(groups):
        load(g).start()

    barrier = pltpu.get_barrier_semaphore()
    others = (1, -1, rotation, -rotation, rotation + 1, -rotation - 1)
    for offset in others:
        pl.semaphore_signal(barrier, inc=1, device_id={"elem": at(offset)}, device_id_type=MESH)

    def copy(x, which, start=0, size=count):
        if which < 2:
            src = u_ref if x == 0 else recv_ref.at[x, pl.ds(2 * count + start, size)]
            dst = recv_ref.at[x, pl.ds(which * count + start, size)]
            target = at(1) if which == 0 else at(-1)
        else:
            src = zsend_ref.at[x, pl.ds(start, size)]
            dst = zrecv_ref.at[x, pl.ds((which - 2) * count + start, size)]
            target = at(-rotation) if which == 2 else at(-rotation - 1)
        return pltpu.make_async_remote_copy(
            src_ref=src, dst_ref=dst, send_sem=send_sem.at[x, which],
            recv_sem=recv_sem.at[x, which], device_id={"elem": target}, device_id_type=MESH,
        )

    def lower_rows(col_ref):
        low = col_ref[strided(0, FIELDS * FACE), :]
        low = jnp.concatenate([low, jnp.zeros((LANES - FIELDS * FACE, LANES), jnp.float32)], axis=0)
        return low.T

    def send(x, vectors, g):
        start = pl.multiple_of(g * GROUP, GROUP)
        low = lower_rows(grp)
        for v in range(vectors):
            zsend_ref[x + v, pl.ds(start, GROUP)] = low[v * GROUP : (v + 1) * GROUP]
        for v in range(vectors):
            copy(x + v, 3, start, GROUP).start()
            copy(x + v, 2, start, GROUP).start()
        rows = grp[...].T
        for v in range(vectors):
            recv_ref[x + v, pl.ds(2 * count + start, GROUP)] = rows[v * GROUP : (v + 1) * GROUP]
        for v in range(vectors):
            copy(x + v, 0, start, GROUP).start()
            copy(x + v, 1, start, GROUP).start()

    u_rows = u_ref[...]
    uc[...] = jnp.concatenate([u_rows] * SECTIONS, axis=0).T
    zsend_ref[0] = lower_rows(uc)[:count]
    recv_ref[0, 2 * count : 3 * count] = u_rows
    pl.semaphore_wait(barrier, len(others))
    copy(0, 3).start()
    copy(0, 2).start()
    copy(0, 0).start()
    copy(0, 1).start()
    to_k_order(uc, uk)
    volume(uc, uk, lc, tk, 1.0)

    lane = lax.broadcasted_iota(jnp.int32, (1, LANES), 1)
    block = lane // count
    local = lane - block * count
    row = lax.broadcasted_iota(jnp.int32, (LANES, 1), 0)

    def ids(*offsets):
        out = jnp.full((LANES, 1), -1, jnp.int32)
        for index, offset in enumerate(offsets):
            inside = (row >= index * count) & (row < (index + 1) * count)
            out = jnp.where(inside, at(offset) * count + row - index * count, out)
        return out

    side_ids = ids(-1, 1, 0)
    sliding_ids = ids(rotation, rotation + 1)
    per_row = LANES // count
    listed = partner_ref[pl.ds(rank // per_row, 1), :]
    partner = jnp.zeros((1, LANES), jnp.int32)
    for index in range(per_row):
        part_row = jnp.concatenate([listed[:, index * count : (index + 1) * count]] * SECTIONS, axis=1)
        partner = jnp.where(rank % per_row == index, part_row, partner)
    for face in range(6):
        if face < 5:
            wanted = jnp.concatenate([nbr_ref[face : face + 1, :]] * SECTIONS, axis=1)
            match = side_ids == wanted
        else:
            match = sliding_ids == partner
        pick_ref[face] = jnp.where(match, 1.0, 0.0).astype(jnp.bfloat16)

    def picked(face, values):
        high = values.astype(jnp.bfloat16)
        rest = values - high.astype(jnp.float32)
        middle = rest.astype(jnp.bfloat16)
        low = (rest - middle.astype(jnp.float32)).astype(jnp.bfloat16)
        split = jnp.concatenate([high, middle, low], axis=0)
        got = lax.dot_general(
            split, pick_ref[face], (((1,), (0,)), ((), ())), preferred_element_type=jnp.float32
        )
        n = values.shape[0]
        return (got[2 * n :] + got[n : 2 * n]) + got[:n]

    def receive(x, put):
        for which in range(4):
            copy(x, which).wait_recv()
        mine = recv_ref[x]
        nc[...] = jnp.concatenate([mine, mine[2 * count :]], axis=0).T
        to_k_order(nc, nk)
        for face in range(5):
            position = (NODE1 - 1) * (1 - face % 2)
            put(face, picked(face, jnp.concatenate(slab(nc, nk, face // 2, position), axis=0)))
        sliding = zrecv_ref[x]
        sliding = jnp.concatenate([sliding, sliding], axis=0).T
        put(5, picked(5, sliding[: FIELDS * FACE]))

    def keep(slot):
        def put(face, value):
            near_ref[slot, face] = value
        return put

    def near(slot):
        def faces(face):
            return [near_ref[slot, face, f * FACE : (f + 1) * FACE, :] for f in range(FIELDS)]
        return faces

    def per_lane(value_of):
        out = jnp.zeros((1, LANES), jnp.float32)
        for group in range(SECTIONS):
            value = jnp.float32(value_of(0, group))
            for other in range(1, parts):
                value = jnp.where(part == other, jnp.float32(value_of(other, group)), value)
            out = jnp.where(block == group, value, out)
        return out

    cycle = lane % GROUP
    eighth = lane // GROUP

    def matvec(dst, vectors, first, x=None):
        dst[...] = jnp.zeros_like(dst)

        @pl.loop(0, groups)
        def _(g):
            if first:
                load(g).wait()
            xs = [
                xr[pl.ds(pl.multiple_of(v * count + g * GROUP, GROUP), GROUP), :]
                for v in range(vectors)
            ]
            for c in range(unknowns // ROWS):
                rows = slice(c * ROWS, (c + 1) * ROWS)
                accs = [jnp.zeros((ROWS, LANES), jnp.float32)] * vectors
                for k in range(GROUP):
                    a = a_ref[g * GROUP + k, rows, :]
                    for v in range(vectors):
                        total = jnp.sum(a * xs[v][k : k + 1, :], axis=1, keepdims=True)
                        accs[v] = jnp.where(cycle == k, total, accs[v])
                full = dst[rows, :]
                for v in range(vectors):
                    if vectors == 1:
                        here = local // GROUP == g
                    else:
                        here = eighth == v * groups + g
                    full = jnp.where(here, accs[v], full)
                dst[rows, :] = full
                if x is not None:
                    mine = accs[0]
                    for v in range(1, vectors):
                        mine = jnp.where(eighth % vectors == v, accs[v], mine)
                    grp[rows, :] = mine
            if x is not None:
                send(x, vectors, g)

    receive(0, keep(0))
    surface(uc, uk, near(0), lc, tk, 1.0)
    xr[...] = lc[...].T
    matvec(vc, 1, True, 1)
    receive(1, keep(1))
    lift(near(1), lc, tk)
    xr[...] = lc[...].T
    matvec(wc, 1, False, 2)

    def alpha(i):
        return time_step * sum(butcher[i])

    def coupling(i):
        return time_step * butcher[i][i] * dissipation * inv_weight

    def own(p, group):
        return p * own_sections + group % own_sections

    alphas = per_lane(lambda p, s: alpha(s))
    betas = per_lane(lambda p, s: alpha(s) * coupling(s))
    gc[...] = uc[...] + alphas * vc[...] + betas * wc[...]
    to_k_order(gc, uk)

    def add(face, value):
        near_ref[0, face] = near_ref[0, face] + alphas * near_ref[1, face] + betas * value

    volume(gc, uk, lc, tk, time_step)
    receive(2, add)
    surface(gc, uk, near(0), lc, tk, time_step)

    own_alphas = per_lane(lambda p, g: alpha(own(p, g)))
    own_betas = per_lane(lambda p, g: alpha(own(p, g)) * coupling(own(p, g)))
    own_couplings = per_lane(lambda p, g: coupling(own(p, g)))
    step = own_alphas * vc[...] + own_betas * wc[...]
    tend = lc[...]
    total = -step
    for shift in range(SECTIONS):
        moved = tend if shift == 0 else pltpu.roll(tend, shift * count, 1)
        weights = per_lane(lambda p, g: butcher[own(p, g)][(g - shift) % SECTIONS])
        total = total + weights * moved
    gc[...] = step
    xr[...] = total.T
    matvec(fc, own_sections, False, 3)
    receive(3, keep(0))
    for s in range(1, own_sections):
        def merge(face, value, s=s):
            near_ref[0, face] = jnp.where(block == s, value, near_ref[0, face])
        receive(3 + s, merge)
    lift(near(0), lc, tk)
    xr[...] = (own_couplings * lc[...]).T
    matvec(wc, own_sections, False)
    rows = (gc[...] + fc[...] + wc[...]).T
    for s in range(own_sections):
        out_ref[s] = rows[s * count : (s + 1) * count]
    for x in range(3 + own_sections):
        for which in range(4):
            copy(x, which).wait_send()


def on_device(u_start, inverses, neighbours, partners):
    count, unknowns = u_start.shape
    devices = lax.axis_size("elem")
    own_sections = SECTIONS // lax.axis_size("section")
    listed = partners.reshape(-1, LANES)
    exchanges = 3 + own_sections
    column = pltpu.VMEM((unknowns, LANES), jnp.float32)
    vmem = pl.BlockSpec(memory_space=pltpu.VMEM)
    change = pl.pallas_call(
        functools.partial(kernel, devices, count),
        out_shape=jax.ShapeDtypeStruct((own_sections, count, unknowns), jnp.float32),
        in_specs=[vmem, vmem, vmem, pl.BlockSpec(memory_space=pl.ANY)],
        out_specs=vmem,
        scratch_shapes=[
            pltpu.VMEM((count, unknowns, unknowns), jnp.float32),
            pltpu.VMEM((exchanges, 3 * count, unknowns), jnp.float32),
            pltpu.VMEM((exchanges, 2 * count, LANES), jnp.float32),
            pltpu.VMEM((exchanges, count, LANES), jnp.float32),
            pltpu.VMEM((6, LANES, LANES), jnp.bfloat16),
            pltpu.VMEM((2, 6, FIELDS * FACE, LANES), jnp.float32),
        ]
        + [column] * 11
        + [
            pltpu.VMEM((LANES, unknowns), jnp.float32),
            pltpu.SemaphoreType.DMA((count // GROUP,)),
            pltpu.SemaphoreType.DMA((exchanges, 4)),
            pltpu.SemaphoreType.DMA((exchanges, 4)),
        ],
        compiler_params=pltpu.CompilerParams(
            collective_id=0, has_side_effects=True, vmem_limit_bytes=60 * 1024 * 1024
        ),
    )(u_start, neighbours.T, listed, inverses)
    return u_start[None] + change


def solution(mesh):
    placed = (P("elem", None), P("elem", None, None), P("elem", None), P())
    return jax.shard_map(
        on_device, mesh=mesh, in_specs=placed, out_specs=P("section", "elem", None), check_vma=False
    )
```

```python
import functools
import math

import jax
import jax.numpy as jnp
from jax import lax
from jax.experimental import pallas as pl
from jax.experimental.pallas import tpu as pltpu
from jax.sharding import PartitionSpec as P

NODE1 = 4
SECTIONS = 4
NEWTON = 2


time_step = 0.03
dissipation = 2.0
enthalpy_factor = 3.5
radau_nodes = [0.08858795951270394, 0.4094668644407347, 0.787659461760847, 1.0]


def lobatto():
    node_count = NODE1
    inner_value = 1.0 / math.sqrt(5.0)
    lobatto_nodes = [-1.0, -inner_value, inner_value, 1.0]
    products = []
    for row in range(node_count):
        value = 1.0
        for other in range(node_count):
            if other != row:
                value = value * (lobatto_nodes[row] - lobatto_nodes[other])
        products.append(value)
    derivative = []
    for row in range(node_count):
        entries = []
        for column in range(node_count):
            if row == column:
                total = 0.0
                for other in range(node_count):
                    if other != row:
                        total = total + 1.0 / (lobatto_nodes[row] - lobatto_nodes[other])
                entries.append(2.0 * total)
            else:
                entries.append(
                    2.0
                    * (products[row] / products[column])
                    / (lobatto_nodes[row] - lobatto_nodes[column])
                )
        derivative.append(entries)
    return derivative, float(node_count * (node_count - 1) / 2.0)


def radau_table():
    section_total = SECTIONS
    butcher = []
    columns = []
    for column in range(section_total):
        coeffs = [1.0]
        scale = 1.0
        for other in range(section_total):
            if other != column:
                shifted = [0.0] + coeffs
                for position in range(len(coeffs)):
                    shifted[position] = shifted[position] - radau_nodes[other] * coeffs[position]
                coeffs = shifted
                scale = scale * (radau_nodes[column] - radau_nodes[other])
        integral = [0.0] + [
            coeffs[position] / (position + 1.0) / scale for position in range(len(coeffs))
        ]
        columns.append(integral)
    for row in range(section_total):
        entries = []
        for column in range(section_total):
            value = 0.0
            for coefficient in reversed(columns[column]):
                value = value * radau_nodes[row] + coefficient
            entries.append(value)
        butcher.append(entries)
    return butcher


FIELDS = 5
NODES = NODE1**3
FACE = NODE1**2
LANES = 128
GROUP = 8
ROWS = 64
MESH = pl.DeviceIdType.MESH


def strided(start, count):
    return pl.ds(start, count, stride=NODE1)


def to_k_order(src_ref, k_ref):
    for field in range(FIELDS):
        for k in range(NODE1):
            base = field * NODES
            k_ref[base + k * FACE : base + (k + 1) * FACE, :] = src_ref[strided(base + k, FACE), :]


def slab(src_ref, k_ref, direction, position):
    out = []
    for field in range(FIELDS):
        base = field * NODES
        if direction == 0:
            out.append(src_ref[base + position * FACE : base + (position + 1) * FACE, :])
        elif direction == 1:
            out.append(k_ref[strided(base + position, FACE), :])
        else:
            out.append(k_ref[base + position * FACE : base + (position + 1) * FACE, :])
    return out


def put_slabs(out_ref, k_ref, direction, slabs):
    for position in range(NODE1):
        for field in range(FIELDS):
            base = field * NODES
            rows = slice(base + position * FACE, base + (position + 1) * FACE)
            value = slabs[position][field]
            if direction == 0:
                out_ref[rows, :] = value
            elif direction == 1:
                k_ref[strided(base + position, FACE), :] = value
            else:
                value = k_ref[rows, :] + value
                there = strided(base + position, FACE)
                out_ref[there, :] = out_ref[there, :] + value


def speed2(state):
    return state[1] * state[1] + state[2] * state[2] + state[3] * state[3]


def two_point(a, ka, b, kb, direction):
    r = a[0] + b[0]
    v = [a[1 + c] + b[1 + c] for c in range(3)]
    p = a[4] + b[4]
    n = v[direction]
    m = (0.25 * r) * n
    half = 0.5 * m
    out = [m]
    for c in range(3):
        term = half * v[c]
        if c == direction:
            term = term + 0.5 * p
        out.append(term)
    out.append((0.25 * enthalpy_factor * p) * n + (0.5 * half) * (ka + kb))
    return out


def volume(uc, uk, out_ref, tk, scale):
    deriv, _ = lobatto()
    for direction in range(3):
        states = [slab(uc, uk, direction, pos) for pos in range(NODE1)]
        speeds = [speed2(state) for state in states]
        sums = [None] * NODE1
        for a in range(NODE1):
            for b in range(a + 1, NODE1):
                f = two_point(states[a], speeds[a], states[b], speeds[b], direction)
                for at, other in ((a, b), (b, a)):
                    c = -2.0 * scale * deriv[at][other]
                    terms = [c * x for x in f]
                    sums[at] = terms if sums[at] is None else [x + y for x, y in zip(sums[at], terms)]
        put_slabs(out_ref, tk, direction, sums)


def surface(uc, uk, faces, out_ref, tk, scale):
    _, inv_weight = lobatto()

    def terms(face):
        direction, upper = face // 2, face % 2
        own = slab(uc, uk, direction, (NODE1 - 1) * upper)
        other = faces(face)
        f = two_point(own, speed2(own), other, speed2(other), direction)
        c = -2.0 * scale * inv_weight
        d = 0.5 * dissipation * c
        sign = 2.0 * upper - 1.0
        return [(c * sign) * x - d * (n - u) for x, n, u in zip(f, other, own)]

    add_faces(terms, out_ref, tk)


def add_faces(terms, out_ref, tk):
    zero = jnp.zeros((FACE, LANES), jnp.float32)
    for face in range(6):
        direction, position = face // 2, (NODE1 - 1) * (face % 2)
        values = terms(face)
        for field in range(FIELDS):
            base = field * NODES
            rows = slice(base + position * FACE, base + (position + 1) * FACE)
            there = strided(base + position, FACE)
            if direction == 0:
                out_ref[rows, :] = out_ref[rows, :] + values[field]
            elif direction == 1:
                tk[there, :] = values[field]
                if face == 3:
                    for inner in range(1, NODE1 - 1):
                        tk[strided(base + inner, FACE), :] = zero
            else:
                tk[rows, :] = tk[rows, :] + values[field]
    for field in range(FIELDS):
        base = field * NODES
        for position in range(NODE1):
            rows = slice(base + position * FACE, base + (position + 1) * FACE)
            there = strided(base + position, FACE)
            out_ref[there, :] = out_ref[there, :] + tk[rows, :]


def lift(faces, out_ref, tk):
    zero = jnp.zeros((FACE, LANES), jnp.float32)
    for direction in range(3):
        slabs = [[zero] * FIELDS for _ in range(NODE1)]
        slabs[0] = faces(2 * direction)
        slabs[NODE1 - 1] = faces(2 * direction + 1)
        put_slabs(out_ref, tk, direction, slabs)


def kernel(
    devices, count, u_in, nbr_in, partner_in, inv_ref, out_ref,
    u_ref, nbr_ref, partner_ref,
    a_ref, recv_ref, zrecv_ref, zsend_ref, pick_ref, near_ref,
    uc, uk, vc, wc, lc, tk, nc, nk, fc, gc, grp, xr,
    in_sem, a_sem, send_sem, recv_sem,
):
    rank = lax.axis_index("elem")
    part = lax.axis_index("section")
    parts = lax.axis_size("section")
    own_sections = SECTIONS // parts
    rotation = devices // 4
    unknowns = FIELDS * NODES
    butcher = radau_table()
    _, inv_weight = lobatto()
    groups = count // GROUP

    def at(offset):
        return lax.rem(rank + (offset + devices), devices)

    def load(g):
        block = pl.ds(g * GROUP, GROUP)
        return pltpu.make_async_copy(inv_ref.at[block], a_ref.at[block], a_sem.at[g])

    barrier = pltpu.get_barrier_semaphore()
    others = (1, -1, rotation, -rotation, rotation + 1, -rotation - 1)
    for offset in others:
        pl.semaphore_signal(barrier, inc=1, device_id={"elem": at(offset)}, device_id_type=MESH)
    small = [
        pltpu.make_async_copy(src, dst, in_sem.at[index])
        for index, (src, dst) in enumerate(
            ((u_in, u_ref), (nbr_in, nbr_ref), (partner_in, partner_ref))
        )
    ]
    for each in small:
        each.start()
    for g in range(groups):
        load(g).start()

    def copy(x, which, start=0, size=count):
        if which < 2:
            src = u_ref if x == 0 else recv_ref.at[x, pl.ds(2 * count + start, size)]
            dst = recv_ref.at[x, pl.ds(which * count + start, size)]
            target = at(1) if which == 0 else at(-1)
        else:
            src = zsend_ref.at[x, pl.ds(start, size)]
            dst = zrecv_ref.at[x, pl.ds((which - 2) * count + start, size)]
            target = at(-rotation) if which == 2 else at(-rotation - 1)
        return pltpu.make_async_remote_copy(
            src_ref=src, dst_ref=dst, send_sem=send_sem.at[x, which],
            recv_sem=recv_sem.at[x, which], device_id={"elem": target}, device_id_type=MESH,
        )

    def lower_rows(col_ref):
        low = col_ref[strided(0, FIELDS * FACE), :]
        low = jnp.concatenate([low, jnp.zeros((LANES - FIELDS * FACE, LANES), jnp.float32)], axis=0)
        return low.T

    def send(x, vectors, g):
        start = pl.multiple_of(g * GROUP, GROUP)
        low = lower_rows(grp)
        for v in range(vectors):
            zsend_ref[x + v, pl.ds(start, GROUP)] = low[v * GROUP : (v + 1) * GROUP]
        for v in range(vectors):
            copy(x + v, 3, start, GROUP).start()
            copy(x + v, 2, start, GROUP).start()
        rows = grp[...].T
        for v in range(vectors):
            recv_ref[x + v, pl.ds(2 * count + start, GROUP)] = rows[v * GROUP : (v + 1) * GROUP]
        for v in range(vectors):
            copy(x + v, 0, start, GROUP).start()
            copy(x + v, 1, start, GROUP).start()

    for each in small:
        each.wait()
    u_rows = u_ref[...]
    uc[...] = jnp.concatenate([u_rows] * SECTIONS, axis=0).T
    zsend_ref[0] = lower_rows(uc)[:count]
    recv_ref[0, 2 * count : 3 * count] = u_rows
    pl.semaphore_wait(barrier, len(others))
    copy(0, 3).start()
    copy(0, 2).start()
    copy(0, 0).start()
    copy(0, 1).start()
    to_k_order(uc, uk)
    volume(uc, uk, lc, tk, 1.0)

    lane = lax.broadcasted_iota(jnp.int32, (1, LANES), 1)
    block = lane // count
    local = lane - block * count
    row = lax.broadcasted_iota(jnp.int32, (LANES, 1), 0)

    def ids(*offsets):
        out = jnp.full((LANES, 1), -1, jnp.int32)
        for index, offset in enumerate(offsets):
            inside = (row >= index * count) & (row < (index + 1) * count)
            out = jnp.where(inside, at(offset) * count + row - index * count, out)
        return out

    side_ids = ids(-1, 1, 0)
    sliding_ids = ids(rotation, rotation + 1)
    per_row = LANES // count
    listed = partner_ref[pl.ds(rank // per_row, 1), :]
    partner = jnp.zeros((1, LANES), jnp.int32)
    for index in range(per_row):
        part_row = jnp.concatenate([listed[:, index * count : (index + 1) * count]] * SECTIONS, axis=1)
        partner = jnp.where(rank % per_row == index, part_row, partner)
    for face in range(6):
        if face < 5:
            wanted = jnp.concatenate([nbr_ref[face : face + 1, :]] * SECTIONS, axis=1)
            match = side_ids == wanted
        else:
            match = sliding_ids == partner
        pick_ref[face] = jnp.where(match, 1.0, 0.0).astype(jnp.bfloat16)

    def picked(face, values):
        high = values.astype(jnp.bfloat16)
        rest = values - high.astype(jnp.float32)
        middle = rest.astype(jnp.bfloat16)
        low = (rest - middle.astype(jnp.float32)).astype(jnp.bfloat16)
        split = jnp.concatenate([high, middle, low], axis=0)
        got = lax.dot_general(
            split, pick_ref[face], (((1,), (0,)), ((), ())), preferred_element_type=jnp.float32
        )
        n = values.shape[0]
        return (got[2 * n :] + got[n : 2 * n]) + got[:n]

    def receive(x, put):
        for which in range(4):
            copy(x, which).wait_recv()
        mine = recv_ref[x]
        nc[...] = jnp.concatenate([mine, mine[2 * count :]], axis=0).T
        to_k_order(nc, nk)
        for face in range(5):
            position = (NODE1 - 1) * (1 - face % 2)
            put(face, picked(face, jnp.concatenate(slab(nc, nk, face // 2, position), axis=0)))
        sliding = zrecv_ref[x]
        sliding = jnp.concatenate([sliding, sliding], axis=0).T
        put(5, picked(5, sliding[: FIELDS * FACE]))

    def keep(slot):
        def put(face, value):
            near_ref[slot, face] = value
        return put

    def near(slot):
        def faces(face):
            return [near_ref[slot, face, f * FACE : (f + 1) * FACE, :] for f in range(FIELDS)]
        return faces

    def per_lane(value_of):
        out = jnp.zeros((1, LANES), jnp.float32)
        for group in range(SECTIONS):
            value = jnp.float32(value_of(0, group))
            for other in range(1, parts):
                value = jnp.where(part == other, jnp.float32(value_of(other, group)), value)
            out = jnp.where(block == group, value, out)
        return out

    cycle = lane % GROUP
    eighth = lane // GROUP

    def matvec(dst, vectors, first, x=None):
        dst[...] = jnp.zeros_like(dst)

        @pl.loop(0, groups)
        def _(g):
            if first:
                load(g).wait()
            xs = [
                xr[pl.ds(pl.multiple_of(v * count + g * GROUP, GROUP), GROUP), :]
                for v in range(vectors)
            ]
            for c in range(unknowns // ROWS):
                rows = slice(c * ROWS, (c + 1) * ROWS)
                accs = [jnp.zeros((ROWS, LANES), jnp.float32)] * vectors
                for k in range(GROUP):
                    a = a_ref[g * GROUP + k, rows, :]
                    for v in range(vectors):
                        total = jnp.sum(a * xs[v][k : k + 1, :], axis=1, keepdims=True)
                        accs[v] = jnp.where(cycle == k, total, accs[v])
                full = dst[rows, :]
                for v in range(vectors):
                    if vectors == 1:
                        here = local // GROUP == g
                    else:
                        here = eighth == v * groups + g
                    full = jnp.where(here, accs[v], full)
                dst[rows, :] = full
                if x is not None:
                    mine = accs[0]
                    for v in range(1, vectors):
                        mine = jnp.where(eighth % vectors == v, accs[v], mine)
                    grp[rows, :] = mine
            if x is not None:
                send(x, vectors, g)

    receive(0, keep(0))
    surface(uc, uk, near(0), lc, tk, 1.0)
    xr[...] = lc[...].T
    matvec(vc, 1, True, 1)
    receive(1, keep(1))
    lift(near(1), lc, tk)
    xr[...] = lc[...].T
    matvec(wc, 1, False, 2)

    def alpha(i):
        return time_step * sum(butcher[i])

    def coupling(i):
        return time_step * butcher[i][i] * dissipation * inv_weight

    def own(p, group):
        return p * own_sections + group % own_sections

    alphas = per_lane(lambda p, s: alpha(s))
    betas = per_lane(lambda p, s: alpha(s) * coupling(s))
    gc[...] = uc[...] + alphas * vc[...] + betas * wc[...]
    to_k_order(gc, uk)

    def add(face, value):
        near_ref[0, face] = near_ref[0, face] + alphas * near_ref[1, face] + betas * value

    volume(gc, uk, lc, tk, time_step)
    receive(2, add)
    surface(gc, uk, near(0), lc, tk, time_step)

    own_alphas = per_lane(lambda p, g: alpha(own(p, g)))
    own_betas = per_lane(lambda p, g: alpha(own(p, g)) * coupling(own(p, g)))
    own_couplings = per_lane(lambda p, g: coupling(own(p, g)))
    step = own_alphas * vc[...] + own_betas * wc[...]
    tend = lc[...]
    total = -step
    for shift in range(SECTIONS):
        moved = tend if shift == 0 else pltpu.roll(tend, shift * count, 1)
        weights = per_lane(lambda p, g: butcher[own(p, g)][(g - shift) % SECTIONS])
        total = total + weights * moved
    gc[...] = step
    xr[...] = total.T
    matvec(fc, own_sections, False, 3)
    receive(3, keep(0))
    for s in range(1, own_sections):
        def merge(face, value, s=s):
            near_ref[0, face] = jnp.where(block == s, value, near_ref[0, face])
        receive(3 + s, merge)
    lift(near(0), lc, tk)
    xr[...] = (own_couplings * lc[...]).T
    matvec(wc, own_sections, False)
    rows = (gc[...] + fc[...] + wc[...]).T
    for s in range(own_sections):
        out_ref[s] = rows[s * count : (s + 1) * count]
    for x in range(3 + own_sections):
        for which in range(4):
            copy(x, which).wait_send()


def on_device(u_start, inverses, neighbours, partners):
    count, unknowns = u_start.shape
    devices = lax.axis_size("elem")
    own_sections = SECTIONS // lax.axis_size("section")
    listed = partners.reshape(-1, LANES)
    exchanges = 3 + own_sections
    column = pltpu.VMEM((unknowns, LANES), jnp.float32)
    vmem = pl.BlockSpec(memory_space=pltpu.VMEM)
    change = pl.pallas_call(
        functools.partial(kernel, devices, count),
        out_shape=jax.ShapeDtypeStruct((own_sections, count, unknowns), jnp.float32),
        in_specs=[pl.BlockSpec(memory_space=pl.ANY)] * 4,
        out_specs=vmem,
        scratch_shapes=[
            pltpu.VMEM(u_start.shape, jnp.float32),
            pltpu.VMEM(neighbours.shape[::-1], jnp.int32),
            pltpu.VMEM(listed.shape, jnp.int32),
            pltpu.VMEM((count, unknowns, unknowns), jnp.float32),
            pltpu.VMEM((exchanges, 3 * count, unknowns), jnp.float32),
            pltpu.VMEM((exchanges, 2 * count, LANES), jnp.float32),
            pltpu.VMEM((exchanges, count, LANES), jnp.float32),
            pltpu.VMEM((6, LANES, LANES), jnp.bfloat16),
            pltpu.VMEM((2, 6, FIELDS * FACE, LANES), jnp.float32),
        ]
        + [column] * 11
        + [
            pltpu.VMEM((LANES, unknowns), jnp.float32),
            pltpu.SemaphoreType.DMA((3,)),
            pltpu.SemaphoreType.DMA((count // GROUP,)),
            pltpu.SemaphoreType.DMA((exchanges, 4)),
            pltpu.SemaphoreType.DMA((exchanges, 4)),
        ],
        compiler_params=pltpu.CompilerParams(
            collective_id=0, has_side_effects=True, vmem_limit_bytes=52 * 1024 * 1024
        ),
    )(u_start, neighbours.T, listed, inverses)
    return u_start[None] + change


def solution(mesh):
    placed = (P("elem", None), P("elem", None, None), P("elem", None), P())
    return jax.shard_map(
        on_device, mesh=mesh, in_specs=placed, out_specs=P("section", "elem", None), check_vma=False
    )
```

```python
import functools
import math

import jax
import jax.numpy as jnp
from jax import lax
from jax.experimental import pallas as pl
from jax.experimental.pallas import tpu as pltpu
from jax.sharding import PartitionSpec as P

NODE1 = 4
SECTIONS = 4
NEWTON = 2


time_step = 0.03
dissipation = 2.0
enthalpy_factor = 3.5
radau_nodes = [0.08858795951270394, 0.4094668644407347, 0.787659461760847, 1.0]


def lobatto():
    node_count = NODE1
    inner_value = 1.0 / math.sqrt(5.0)
    lobatto_nodes = [-1.0, -inner_value, inner_value, 1.0]
    products = []
    for row in range(node_count):
        value = 1.0
        for other in range(node_count):
            if other != row:
                value = value * (lobatto_nodes[row] - lobatto_nodes[other])
        products.append(value)
    derivative = []
    for row in range(node_count):
        entries = []
        for column in range(node_count):
            if row == column:
                total = 0.0
                for other in range(node_count):
                    if other != row:
                        total = total + 1.0 / (lobatto_nodes[row] - lobatto_nodes[other])
                entries.append(2.0 * total)
            else:
                entries.append(
                    2.0
                    * (products[row] / products[column])
                    / (lobatto_nodes[row] - lobatto_nodes[column])
                )
        derivative.append(entries)
    return derivative, float(node_count * (node_count - 1) / 2.0)


def radau_table():
    section_total = SECTIONS
    butcher = []
    columns = []
    for column in range(section_total):
        coeffs = [1.0]
        scale = 1.0
        for other in range(section_total):
            if other != column:
                shifted = [0.0] + coeffs
                for position in range(len(coeffs)):
                    shifted[position] = shifted[position] - radau_nodes[other] * coeffs[position]
                coeffs = shifted
                scale = scale * (radau_nodes[column] - radau_nodes[other])
        integral = [0.0] + [
            coeffs[position] / (position + 1.0) / scale for position in range(len(coeffs))
        ]
        columns.append(integral)
    for row in range(section_total):
        entries = []
        for column in range(section_total):
            value = 0.0
            for coefficient in reversed(columns[column]):
                value = value * radau_nodes[row] + coefficient
            entries.append(value)
        butcher.append(entries)
    return butcher


FIELDS = 5
NODES = NODE1**3
FACE = NODE1**2
LANES = 128
GROUP = 8
ROWS = 64
MESH = pl.DeviceIdType.MESH


def strided(start, count):
    return pl.ds(start, count, stride=NODE1)


def to_k_order(src_ref, k_ref):
    for field in range(FIELDS):
        for k in range(NODE1):
            base = field * NODES
            k_ref[base + k * FACE : base + (k + 1) * FACE, :] = src_ref[strided(base + k, FACE), :]


def slab(src_ref, k_ref, direction, position):
    out = []
    for field in range(FIELDS):
        base = field * NODES
        if direction == 0:
            out.append(src_ref[base + position * FACE : base + (position + 1) * FACE, :])
        elif direction == 1:
            out.append(k_ref[strided(base + position, FACE), :])
        else:
            out.append(k_ref[base + position * FACE : base + (position + 1) * FACE, :])
    return out


def put_slabs(out_ref, k_ref, direction, slabs):
    for position in range(NODE1):
        for field in range(FIELDS):
            base = field * NODES
            rows = slice(base + position * FACE, base + (position + 1) * FACE)
            value = slabs[position][field]
            if direction == 0:
                out_ref[rows, :] = value
            elif direction == 1:
                k_ref[strided(base + position, FACE), :] = value
            else:
                value = k_ref[rows, :] + value
                there = strided(base + position, FACE)
                out_ref[there, :] = out_ref[there, :] + value


def speed2(state):
    return state[1] * state[1] + state[2] * state[2] + state[3] * state[3]


def two_point(a, ka, b, kb, direction):
    r = a[0] + b[0]
    v = [a[1 + c] + b[1 + c] for c in range(3)]
    p = a[4] + b[4]
    n = v[direction]
    m = (0.25 * r) * n
    half = 0.5 * m
    out = [m]
    for c in range(3):
        term = half * v[c]
        if c == direction:
            term = term + 0.5 * p
        out.append(term)
    out.append((0.25 * enthalpy_factor * p) * n + (0.5 * half) * (ka + kb))
    return out


def volume(uc, uk, out_ref, tk, scale):
    deriv, _ = lobatto()
    for direction in range(3):
        states = [slab(uc, uk, direction, pos) for pos in range(NODE1)]
        speeds = [speed2(state) for state in states]
        sums = [None] * NODE1
        for a in range(NODE1):
            for b in range(a + 1, NODE1):
                f = two_point(states[a], speeds[a], states[b], speeds[b], direction)
                for at, other in ((a, b), (b, a)):
                    c = -2.0 * scale * deriv[at][other]
                    terms = [c * x for x in f]
                    sums[at] = terms if sums[at] is None else [x + y for x, y in zip(sums[at], terms)]
        put_slabs(out_ref, tk, direction, sums)


def surface(uc, uk, faces, out_ref, tk, scale):
    _, inv_weight = lobatto()

    def terms(face):
        direction, upper = face // 2, face % 2
        own = slab(uc, uk, direction, (NODE1 - 1) * upper)
        other = faces(face)
        f = two_point(own, speed2(own), other, speed2(other), direction)
        c = -2.0 * scale * inv_weight
        d = 0.5 * dissipation * c
        sign = 2.0 * upper - 1.0
        return [(c * sign) * x - d * (n - u) for x, n, u in zip(f, other, own)]

    add_faces(terms, out_ref, tk)


def add_faces(terms, out_ref, tk):
    zero = jnp.zeros((FACE, LANES), jnp.float32)
    for face in range(6):
        direction, position = face // 2, (NODE1 - 1) * (face % 2)
        values = terms(face)
        for field in range(FIELDS):
            base = field * NODES
            rows = slice(base + position * FACE, base + (position + 1) * FACE)
            there = strided(base + position, FACE)
            if direction == 0:
                out_ref[rows, :] = out_ref[rows, :] + values[field]
            elif direction == 1:
                tk[there, :] = values[field]
                if face == 3:
                    for inner in range(1, NODE1 - 1):
                        tk[strided(base + inner, FACE), :] = zero
            else:
                tk[rows, :] = tk[rows, :] + values[field]
    for field in range(FIELDS):
        base = field * NODES
        for position in range(NODE1):
            rows = slice(base + position * FACE, base + (position + 1) * FACE)
            there = strided(base + position, FACE)
            out_ref[there, :] = out_ref[there, :] + tk[rows, :]


def lift(faces, out_ref, tk):
    zero = jnp.zeros((FACE, LANES), jnp.float32)
    for direction in range(3):
        slabs = [[zero] * FIELDS for _ in range(NODE1)]
        slabs[0] = faces(2 * direction)
        slabs[NODE1 - 1] = faces(2 * direction + 1)
        put_slabs(out_ref, tk, direction, slabs)


def kernel(
    devices, count, u_in, nbr_in, partner_in, inv_ref, out_ref,
    u_ref, nbr_ref, partner_ref,
    a_ref, recv_ref, zrecv_ref, zsend_ref, pick_ref, near_ref,
    uc, uk, vc, wc, lc, tk, nc, nk, fc, gc, grp, xr,
    in_sem, a_sem, send_sem, recv_sem,
):
    rank = lax.axis_index("elem")
    part = lax.axis_index("section")
    parts = lax.axis_size("section")
    own_sections = SECTIONS // parts
    rotation = devices // 4
    unknowns = FIELDS * NODES
    butcher = radau_table()
    _, inv_weight = lobatto()
    groups = count // GROUP

    def at(offset):
        return lax.rem(rank + (offset + devices), devices)

    def load(g):
        block = pl.ds(g * GROUP, GROUP)
        return pltpu.make_async_copy(inv_ref.at[block], a_ref.at[block], a_sem.at[g])

    barrier = pltpu.get_barrier_semaphore()
    others = (1, -1, rotation, -rotation, rotation + 1, -rotation - 1)
    for offset in others:
        pl.semaphore_signal(barrier, inc=1, device_id={"elem": at(offset)}, device_id_type=MESH)
    small = [
        pltpu.make_async_copy(src, dst, in_sem.at[index])
        for index, (src, dst) in enumerate(
            ((u_in, u_ref), (nbr_in, nbr_ref), (partner_in, partner_ref))
        )
    ]
    for each in small:
        each.start()
    for g in range(groups):
        load(g).start()

    def copy(x, which, start=0, size=count):
        if which < 2:
            src = u_ref if x == 0 else recv_ref.at[x, pl.ds(2 * count + start, size)]
            dst = recv_ref.at[x, pl.ds(which * count + start, size)]
            target = at(1) if which == 0 else at(-1)
        else:
            src = zsend_ref.at[x, pl.ds(start, size)]
            dst = zrecv_ref.at[x, pl.ds((which - 2) * count + start, size)]
            target = at(-rotation) if which == 2 else at(-rotation - 1)
        return pltpu.make_async_remote_copy(
            src_ref=src, dst_ref=dst, send_sem=send_sem.at[x, which],
            recv_sem=recv_sem.at[x, which], device_id={"elem": target}, device_id_type=MESH,
        )

    def lower_rows(col_ref):
        low = col_ref[strided(0, FIELDS * FACE), :]
        low = jnp.concatenate([low, jnp.zeros((LANES - FIELDS * FACE, LANES), jnp.float32)], axis=0)
        return low.T

    def send(x, vectors, g):
        start = pl.multiple_of(g * GROUP, GROUP)
        low = lower_rows(grp)
        for v in range(vectors):
            zsend_ref[x + v, pl.ds(start, GROUP)] = low[v * GROUP : (v + 1) * GROUP]
        for v in range(vectors):
            copy(x + v, 3, start, GROUP).start()
            copy(x + v, 2, start, GROUP).start()
        rows = grp[...].T
        for v in range(vectors):
            recv_ref[x + v, pl.ds(2 * count + start, GROUP)] = rows[v * GROUP : (v + 1) * GROUP]
        for v in range(vectors):
            copy(x + v, 0, start, GROUP).start()
            copy(x + v, 1, start, GROUP).start()

    for each in small:
        each.wait()
    u_rows = u_ref[...]
    uc[...] = jnp.concatenate([u_rows] * SECTIONS, axis=0).T
    zsend_ref[0] = lower_rows(uc)[:count]
    recv_ref[0, 2 * count : 3 * count] = u_rows
    pl.semaphore_wait(barrier, len(others))
    copy(0, 3).start()
    copy(0, 2).start()
    copy(0, 0).start()
    copy(0, 1).start()
    to_k_order(uc, uk)
    volume(uc, uk, lc, tk, 1.0)

    lane = lax.broadcasted_iota(jnp.int32, (1, LANES), 1)
    block = lane // count
    local = lane - block * count
    row = lax.broadcasted_iota(jnp.int32, (LANES, 1), 0)

    def ids(*offsets):
        out = jnp.full((LANES, 1), -1, jnp.int32)
        for index, offset in enumerate(offsets):
            inside = (row >= index * count) & (row < (index + 1) * count)
            out = jnp.where(inside, at(offset) * count + row - index * count, out)
        return out

    side_ids = ids(-1, 1, 0)
    sliding_ids = ids(rotation, rotation + 1)
    per_row = LANES // count
    listed = partner_ref[pl.ds(rank // per_row, 1), :]
    partner = jnp.zeros((1, LANES), jnp.int32)
    for index in range(per_row):
        part_row = jnp.concatenate([listed[:, index * count : (index + 1) * count]] * SECTIONS, axis=1)
        partner = jnp.where(rank % per_row == index, part_row, partner)
    for face in range(6):
        if face < 5:
            wanted = jnp.concatenate([nbr_ref[face : face + 1, :]] * SECTIONS, axis=1)
            match = side_ids == wanted
        else:
            match = sliding_ids == partner
        pick_ref[face] = jnp.where(match, 1.0, 0.0).astype(jnp.bfloat16)

    def picked(face, values):
        high = values.astype(jnp.bfloat16)
        rest = values - high.astype(jnp.float32)
        middle = rest.astype(jnp.bfloat16)
        low = (rest - middle.astype(jnp.float32)).astype(jnp.bfloat16)
        split = jnp.concatenate([high, middle, low], axis=0)
        got = lax.dot_general(
            split, pick_ref[face], (((1,), (0,)), ((), ())), preferred_element_type=jnp.float32
        )
        n = values.shape[0]
        return (got[2 * n :] + got[n : 2 * n]) + got[:n]

    def receive(x, put):
        for which in range(4):
            copy(x, which).wait_recv()
        mine = recv_ref[x]
        nc[...] = jnp.concatenate([mine, mine[2 * count :]], axis=0).T
        to_k_order(nc, nk)
        for face in range(5):
            position = (NODE1 - 1) * (1 - face % 2)
            put(face, picked(face, jnp.concatenate(slab(nc, nk, face // 2, position), axis=0)))
        sliding = zrecv_ref[x]
        sliding = jnp.concatenate([sliding, sliding], axis=0).T
        put(5, picked(5, sliding[: FIELDS * FACE]))

    def keep(slot):
        def put(face, value):
            near_ref[slot, face] = value
        return put

    def near(slot):
        def faces(face):
            return [near_ref[slot, face, f * FACE : (f + 1) * FACE, :] for f in range(FIELDS)]
        return faces

    def per_lane(value_of):
        out = jnp.zeros((1, LANES), jnp.float32)
        for group in range(SECTIONS):
            value = jnp.float32(value_of(0, group))
            for other in range(1, parts):
                value = jnp.where(part == other, jnp.float32(value_of(other, group)), value)
            out = jnp.where(block == group, value, out)
        return out

    cycle = lane % GROUP
    eighth = lane // GROUP

    def matvec(dst, vectors, first, x=None):
        dst[...] = jnp.zeros_like(dst)

        @pl.loop(0, groups)
        def _(g):
            if first:
                load(g).wait()
            xs = [
                xr[pl.ds(pl.multiple_of(v * count + g * GROUP, GROUP), GROUP), :]
                for v in range(vectors)
            ]
            for c in range(unknowns // ROWS):
                rows = slice(c * ROWS, (c + 1) * ROWS)
                accs = [jnp.zeros((ROWS, LANES), jnp.float32)] * vectors
                for k in range(GROUP):
                    a = a_ref[g * GROUP + k, rows, :]
                    for v in range(vectors):
                        total = jnp.sum(a * xs[v][k : k + 1, :], axis=1, keepdims=True)
                        accs[v] = jnp.where(cycle == k, total, accs[v])
                full = dst[rows, :]
                for v in range(vectors):
                    if vectors == 1:
                        here = local // GROUP == g
                    else:
                        here = eighth == v * groups + g
                    full = jnp.where(here, accs[v], full)
                dst[rows, :] = full
                if x is not None:
                    mine = accs[0]
                    for v in range(1, vectors):
                        mine = jnp.where(eighth % vectors == v, accs[v], mine)
                    grp[rows, :] = mine
            if x is not None:
                send(x, vectors, g)

    receive(0, keep(0))
    surface(uc, uk, near(0), lc, tk, 1.0)
    xr[...] = lc[...].T
    matvec(vc, 1, True, 1)
    receive(1, keep(1))
    lift(near(1), lc, tk)
    xr[...] = lc[...].T
    matvec(wc, 1, False, 2)

    def alpha(i):
        return time_step * sum(butcher[i])

    def coupling(i):
        return time_step * butcher[i][i] * dissipation * inv_weight

    def own(p, group):
        return p * own_sections + group % own_sections

    alphas = per_lane(lambda p, s: alpha(s))
    betas = per_lane(lambda p, s: alpha(s) * coupling(s))
    gc[...] = uc[...] + alphas * vc[...] + betas * wc[...]
    to_k_order(gc, uk)

    def add(face, value):
        near_ref[0, face] = near_ref[0, face] + alphas * near_ref[1, face] + betas * value

    volume(gc, uk, lc, tk, time_step)
    receive(2, add)
    surface(gc, uk, near(0), lc, tk, time_step)

    own_alphas = per_lane(lambda p, g: alpha(own(p, g)))
    own_betas = per_lane(lambda p, g: alpha(own(p, g)) * coupling(own(p, g)))
    own_couplings = per_lane(lambda p, g: coupling(own(p, g)))
    step = own_alphas * vc[...] + own_betas * wc[...]
    tend = lc[...]
    total = -step
    for shift in range(SECTIONS):
        moved = tend if shift == 0 else pltpu.roll(tend, shift * count, 1)
        weights = per_lane(lambda p, g: butcher[own(p, g)][(g - shift) % SECTIONS])
        total = total + weights * moved
    gc[...] = step
    xr[...] = total.T
    matvec(fc, own_sections, False, 3)
    receive(3, keep(0))
    for s in range(1, own_sections):
        def merge(face, value, s=s):
            near_ref[0, face] = jnp.where(block == s, value, near_ref[0, face])
        receive(3 + s, merge)
    lift(near(0), lc, tk)
    xr[...] = (own_couplings * lc[...]).T
    matvec(wc, own_sections, False)
    rows = (gc[...] + fc[...] + wc[...]).T
    for s in range(own_sections):
        out_ref[s] = rows[s * count : (s + 1) * count]
    for x in range(3 + own_sections):
        for which in range(4):
            copy(x, which).wait_send()


def on_device(u_start, inverses, neighbours, partners):
    count, unknowns = u_start.shape
    devices = lax.axis_size("elem")
    own_sections = SECTIONS // lax.axis_size("section")
    listed = partners.reshape(-1, LANES)
    exchanges = 3 + own_sections
    column = pltpu.VMEM((unknowns, LANES), jnp.float32)
    vmem = pl.BlockSpec(memory_space=pltpu.VMEM)
    change = pl.pallas_call(
        functools.partial(kernel, devices, count),
        out_shape=jax.ShapeDtypeStruct((own_sections, count, unknowns), jnp.float32),
        in_specs=[pl.BlockSpec(memory_space=pl.ANY)] * 4,
        out_specs=vmem,
        scratch_shapes=[
            pltpu.VMEM(u_start.shape, jnp.float32),
            pltpu.VMEM(neighbours.shape[::-1], jnp.int32),
            pltpu.VMEM(listed.shape, jnp.int32),
            pltpu.VMEM((count, unknowns, unknowns), jnp.float32),
            pltpu.VMEM((exchanges, 3 * count, unknowns), jnp.float32),
            pltpu.VMEM((exchanges, 2 * count, LANES), jnp.float32),
            pltpu.VMEM((exchanges, count, LANES), jnp.float32),
            pltpu.VMEM((6, LANES, LANES), jnp.bfloat16),
            pltpu.VMEM((2, 6, FIELDS * FACE, LANES), jnp.float32),
        ]
        + [column] * 11
        + [
            pltpu.VMEM((LANES, unknowns), jnp.float32),
            pltpu.SemaphoreType.DMA((3,)),
            pltpu.SemaphoreType.DMA((count // GROUP,)),
            pltpu.SemaphoreType.DMA((exchanges, 4)),
            pltpu.SemaphoreType.DMA((exchanges, 4)),
        ],
        compiler_params=pltpu.CompilerParams(
            collective_id=0, has_side_effects=True, vmem_limit_bytes=67_043_328
        ),
    )(u_start, neighbours.T, listed, inverses)
    return u_start[None] + change


def solution(mesh):
    placed = (P("elem", None), P("elem", None, None), P("elem", None), P())
    return jax.shard_map(
        on_device, mesh=mesh, in_specs=placed, out_specs=P("section", "elem", None), check_vma=False
    )
```

```python
import functools
import math

import jax
import jax.numpy as jnp
from jax import lax
from jax.experimental import pallas as pl
from jax.experimental.pallas import tpu as pltpu
from jax.sharding import PartitionSpec as P

NODE1 = 4
SECTIONS = 4
NEWTON = 2


time_step = 0.03
dissipation = 2.0
enthalpy_factor = 3.5
radau_nodes = [0.08858795951270394, 0.4094668644407347, 0.787659461760847, 1.0]


def lobatto():
    node_count = NODE1
    inner_value = 1.0 / math.sqrt(5.0)
    lobatto_nodes = [-1.0, -inner_value, inner_value, 1.0]
    products = []
    for row in range(node_count):
        value = 1.0
        for other in range(node_count):
            if other != row:
                value = value * (lobatto_nodes[row] - lobatto_nodes[other])
        products.append(value)
    derivative = []
    for row in range(node_count):
        entries = []
        for column in range(node_count):
            if row == column:
                total = 0.0
                for other in range(node_count):
                    if other != row:
                        total = total + 1.0 / (lobatto_nodes[row] - lobatto_nodes[other])
                entries.append(2.0 * total)
            else:
                entries.append(
                    2.0
                    * (products[row] / products[column])
                    / (lobatto_nodes[row] - lobatto_nodes[column])
                )
        derivative.append(entries)
    return derivative, float(node_count * (node_count - 1) / 2.0)


def radau_table():
    section_total = SECTIONS
    butcher = []
    columns = []
    for column in range(section_total):
        coeffs = [1.0]
        scale = 1.0
        for other in range(section_total):
            if other != column:
                shifted = [0.0] + coeffs
                for position in range(len(coeffs)):
                    shifted[position] = shifted[position] - radau_nodes[other] * coeffs[position]
                coeffs = shifted
                scale = scale * (radau_nodes[column] - radau_nodes[other])
        integral = [0.0] + [
            coeffs[position] / (position + 1.0) / scale for position in range(len(coeffs))
        ]
        columns.append(integral)
    for row in range(section_total):
        entries = []
        for column in range(section_total):
            value = 0.0
            for coefficient in reversed(columns[column]):
                value = value * radau_nodes[row] + coefficient
            entries.append(value)
        butcher.append(entries)
    return butcher


FIELDS = 5
NODES = NODE1**3
FACE = NODE1**2
LANES = 128
GROUP = 8
ROWS = 64
MATRIX = 3
MESH = pl.DeviceIdType.MESH


def strided(start, count):
    return pl.ds(start, count, stride=NODE1)


def to_k_order(src_ref, k_ref):
    for field in range(FIELDS):
        for k in range(NODE1):
            base = field * NODES
            k_ref[base + k * FACE : base + (k + 1) * FACE, :] = src_ref[strided(base + k, FACE), :]


def slab(src_ref, k_ref, direction, position):
    out = []
    for field in range(FIELDS):
        base = field * NODES
        if direction == 0:
            out.append(src_ref[base + position * FACE : base + (position + 1) * FACE, :])
        elif direction == 1:
            out.append(k_ref[strided(base + position, FACE), :])
        else:
            out.append(k_ref[base + position * FACE : base + (position + 1) * FACE, :])
    return out


def put_slabs(out_ref, k_ref, direction, slabs):
    for position in range(NODE1):
        for field in range(FIELDS):
            base = field * NODES
            rows = slice(base + position * FACE, base + (position + 1) * FACE)
            value = slabs[position][field]
            if direction == 0:
                out_ref[rows, :] = value
            elif direction == 1:
                k_ref[strided(base + position, FACE), :] = value
            else:
                value = k_ref[rows, :] + value
                there = strided(base + position, FACE)
                out_ref[there, :] = out_ref[there, :] + value


def speed2(state):
    return state[1] * state[1] + state[2] * state[2] + state[3] * state[3]


def two_point(a, ka, b, kb, direction):
    r = a[0] + b[0]
    v = [a[1 + c] + b[1 + c] for c in range(3)]
    p = a[4] + b[4]
    n = v[direction]
    m = (0.25 * r) * n
    half = 0.5 * m
    out = [m]
    for c in range(3):
        term = half * v[c]
        if c == direction:
            term = term + 0.5 * p
        out.append(term)
    out.append((0.25 * enthalpy_factor * p) * n + (0.5 * half) * (ka + kb))
    return out


def volume(uc, uk, out_ref, tk, scale):
    deriv, _ = lobatto()
    for direction in range(3):
        states = [slab(uc, uk, direction, pos) for pos in range(NODE1)]
        speeds = [speed2(state) for state in states]
        sums = [None] * NODE1
        for a in range(NODE1):
            for b in range(a + 1, NODE1):
                f = two_point(states[a], speeds[a], states[b], speeds[b], direction)
                for at, other in ((a, b), (b, a)):
                    c = -2.0 * scale * deriv[at][other]
                    terms = [c * x for x in f]
                    sums[at] = terms if sums[at] is None else [x + y for x, y in zip(sums[at], terms)]
        put_slabs(out_ref, tk, direction, sums)


def surface(uc, uk, faces, out_ref, tk, scale):
    _, inv_weight = lobatto()

    def terms(face):
        direction, upper = face // 2, face % 2
        own = slab(uc, uk, direction, (NODE1 - 1) * upper)
        other = faces(face)
        f = two_point(own, speed2(own), other, speed2(other), direction)
        c = -2.0 * scale * inv_weight
        d = 0.5 * dissipation * c
        sign = 2.0 * upper - 1.0
        return [(c * sign) * x - d * (n - u) for x, n, u in zip(f, other, own)]

    add_faces(terms, out_ref, tk)


def add_faces(terms, out_ref, tk):
    zero = jnp.zeros((FACE, LANES), jnp.float32)
    for face in range(6):
        direction, position = face // 2, (NODE1 - 1) * (face % 2)
        values = terms(face)
        for field in range(FIELDS):
            base = field * NODES
            rows = slice(base + position * FACE, base + (position + 1) * FACE)
            there = strided(base + position, FACE)
            if direction == 0:
                out_ref[rows, :] = out_ref[rows, :] + values[field]
            elif direction == 1:
                tk[there, :] = values[field]
                if face == 3:
                    for inner in range(1, NODE1 - 1):
                        tk[strided(base + inner, FACE), :] = zero
            else:
                tk[rows, :] = tk[rows, :] + values[field]
    for field in range(FIELDS):
        base = field * NODES
        for position in range(NODE1):
            rows = slice(base + position * FACE, base + (position + 1) * FACE)
            there = strided(base + position, FACE)
            out_ref[there, :] = out_ref[there, :] + tk[rows, :]


def lift(faces, out_ref, tk):
    zero = jnp.zeros((FACE, LANES), jnp.float32)
    for direction in range(3):
        slabs = [[zero] * FIELDS for _ in range(NODE1)]
        slabs[0] = faces(2 * direction)
        slabs[NODE1 - 1] = faces(2 * direction + 1)
        put_slabs(out_ref, tk, direction, slabs)


def kernel(
    devices, count, u_in, nbr_in, partner_in, inv_ref, out_ref,
    u_ref, nbr_ref, partner_ref,
    a_ref, recv_ref, zrecv_ref, zsend_ref, pick_ref, near_ref,
    uc, uk, vc, wc, lc, tk, nc, nk, fc, gc, all_rows, low_rows, half_ref, w_ref, dot_ref, xr,
    in_sem, a_sem, send_sem, recv_sem,
):
    rank = lax.axis_index("elem")
    part = lax.axis_index("section")
    parts = lax.axis_size("section")
    own_sections = SECTIONS // parts
    rotation = devices // 4
    unknowns = FIELDS * NODES
    butcher = radau_table()
    _, inv_weight = lobatto()
    groups = count // GROUP

    def at(offset):
        return lax.rem(rank + (offset + devices), devices)

    def load(g):
        block = pl.ds(g * GROUP, GROUP)
        return pltpu.make_async_copy(inv_ref.at[block], a_ref.at[block], a_sem.at[g])

    barrier = pltpu.get_barrier_semaphore()
    others = (1, -1, rotation, -rotation, rotation + 1, -rotation - 1)
    for offset in others:
        pl.semaphore_signal(barrier, inc=1, device_id={"elem": at(offset)}, device_id_type=MESH)
    small = [
        pltpu.make_async_copy(src, dst, in_sem.at[index])
        for index, (src, dst) in enumerate(
            ((u_in, u_ref), (nbr_in, nbr_ref), (partner_in, partner_ref))
        )
    ]
    for each in small:
        each.start()
    for g in range(groups):
        load(g).start()

    def copy(x, which, start=0, size=count):
        if which < 2:
            src = u_ref if x == 0 else recv_ref.at[x, pl.ds(2 * count + start, size)]
            dst = recv_ref.at[x, pl.ds(which * count + start, size)]
            target = at(1) if which == 0 else at(-1)
        else:
            src = zsend_ref.at[x, pl.ds(start, size)]
            dst = zrecv_ref.at[x, pl.ds((which - 2) * count + start, size)]
            target = at(-rotation) if which == 2 else at(-rotation - 1)
        return pltpu.make_async_remote_copy(
            src_ref=src, dst_ref=dst, send_sem=send_sem.at[x, which],
            recv_sem=recv_sem.at[x, which], device_id={"elem": target}, device_id_type=MESH,
        )

    def lower_rows(col_ref):
        low = col_ref[strided(0, FIELDS * FACE), :]
        low = jnp.concatenate([low, jnp.zeros((LANES - FIELDS * FACE, LANES), jnp.float32)], axis=0)
        return low.T

    def send(x, vectors, g, dst):
        start = pl.multiple_of(g * GROUP, GROUP)
        low_rows[...] = lower_rows(dst)
        all_rows[...] = dst[...].T
        for v in range(vectors):
            zsend_ref[x + v, pl.ds(start, GROUP)] = low_rows[pl.ds(v * count + start, GROUP), :]
        for v in range(vectors):
            copy(x + v, 3, start, GROUP).start()
            copy(x + v, 2, start, GROUP).start()
        for v in range(vectors):
            recv_ref[x + v, pl.ds(2 * count + start, GROUP)] = all_rows[pl.ds(v * count + start, GROUP), :]
        for v in range(vectors):
            copy(x + v, 0, start, GROUP).start()
            copy(x + v, 1, start, GROUP).start()

    for each in small:
        each.wait()
    u_rows = u_ref[...]
    uc[...] = jnp.concatenate([u_rows] * SECTIONS, axis=0).T
    zsend_ref[0] = lower_rows(uc)[:count]
    recv_ref[0, 2 * count : 3 * count] = u_rows
    pl.semaphore_wait(barrier, len(others))
    copy(0, 3).start()
    copy(0, 2).start()
    copy(0, 0).start()
    copy(0, 1).start()
    to_k_order(uc, uk)
    volume(uc, uk, lc, tk, 1.0)

    lane = lax.broadcasted_iota(jnp.int32, (1, LANES), 1)
    block = lane // count
    local = lane - block * count
    row = lax.broadcasted_iota(jnp.int32, (LANES, 1), 0)

    def ids(*offsets):
        out = jnp.full((LANES, 1), -1, jnp.int32)
        for index, offset in enumerate(offsets):
            inside = (row >= index * count) & (row < (index + 1) * count)
            out = jnp.where(inside, at(offset) * count + row - index * count, out)
        return out

    side_ids = ids(-1, 1, 0)
    sliding_ids = ids(rotation, rotation + 1)
    per_row = LANES // count
    listed = partner_ref[pl.ds(rank // per_row, 1), :]
    partner = jnp.zeros((1, LANES), jnp.int32)
    for index in range(per_row):
        part_row = jnp.concatenate([listed[:, index * count : (index + 1) * count]] * SECTIONS, axis=1)
        partner = jnp.where(rank % per_row == index, part_row, partner)
    for face in range(6):
        if face < 5:
            wanted = jnp.concatenate([nbr_ref[face : face + 1, :]] * SECTIONS, axis=1)
            match = side_ids == wanted
        else:
            match = sliding_ids == partner
        pick_ref[face] = jnp.where(match, 1.0, 0.0).astype(jnp.bfloat16)

    def picked(face, values):
        high = values.astype(jnp.bfloat16)
        rest = values - high.astype(jnp.float32)
        middle = rest.astype(jnp.bfloat16)
        low = (rest - middle.astype(jnp.float32)).astype(jnp.bfloat16)
        split = jnp.concatenate([high, middle, low], axis=0)
        got = lax.dot_general(
            split, pick_ref[face], (((1,), (0,)), ((), ())), preferred_element_type=jnp.float32
        )
        n = values.shape[0]
        return (got[2 * n :] + got[n : 2 * n]) + got[:n]

    def receive(x, put):
        for which in range(4):
            copy(x, which).wait_recv()
        mine = recv_ref[x]
        nc[...] = jnp.concatenate([mine, mine[2 * count :]], axis=0).T
        to_k_order(nc, nk)
        for face in range(5):
            position = (NODE1 - 1) * (1 - face % 2)
            put(face, picked(face, jnp.concatenate(slab(nc, nk, face // 2, position), axis=0)))
        sliding = zrecv_ref[x]
        sliding = jnp.concatenate([sliding, sliding], axis=0).T
        put(5, picked(5, sliding[: FIELDS * FACE]))

    def keep(slot):
        def put(face, value):
            near_ref[slot, face] = value
        return put

    def near(slot):
        def faces(face):
            return [near_ref[slot, face, f * FACE : (f + 1) * FACE, :] for f in range(FIELDS)]
        return faces

    def per_lane(value_of):
        out = jnp.zeros((1, LANES), jnp.float32)
        for group in range(SECTIONS):
            value = jnp.float32(value_of(0, group))
            for other in range(1, parts):
                value = jnp.where(part == other, jnp.float32(value_of(other, group)), value)
            out = jnp.where(block == group, value, out)
        return out

    cycle = lane % GROUP
    eighth = lane // GROUP

    def stacked(high, low, axis):
        cut = 2 * LANES
        parts_of = [lax.slice_in_dim(t, 0, cut, axis=axis) for t in (high, low)]
        parts_of += [lax.slice_in_dim(t, cut, unknowns, axis=axis) for t in (high, low)]
        return jnp.concatenate(parts_of, axis=axis)

    def halves():
        @pl.loop(0, groups)
        def _(g):
            load(g).wait()
            for k in range(MATRIX):
                for c in range(unknowns // ROWS):
                    a = a_ref[g * GROUP + GROUP - MATRIX + k, c * ROWS : (c + 1) * ROWS, :]
                    high = a.astype(jnp.bfloat16).astype(jnp.float32)
                    to = k * unknowns + c * ROWS
                    both = stacked(high, a - high, 1)
                    half_ref[g, to : to + ROWS, :] = both.astype(jnp.bfloat16)

    def operand(value):
        xr[...] = value.T
        high = value.astype(jnp.bfloat16).astype(jnp.float32)
        low = pltpu.roll(value - high, LANES // 2, 1)
        both = jnp.where(lane < LANES // 2, high, low)
        w_ref[...] = stacked(both, both, 0).astype(jnp.bfloat16)

    def matvec(dst, vectors, x=None):
        dst[...] = jnp.zeros_like(dst)
        vector_part = GROUP - MATRIX if vectors == 2 else GROUP

        @pl.loop(0, groups)
        def _(g):
            if vectors == 2:
                dot_ref[...] = jnp.dot(
                    half_ref[g], w_ref[...], preferred_element_type=jnp.float32
                )
            xs = [
                xr[pl.ds(pl.multiple_of(v * count + g * GROUP, GROUP), GROUP), :]
                for v in range(vectors)
            ]
            for c in range(unknowns // ROWS):
                rows = slice(c * ROWS, (c + 1) * ROWS)
                accs = [jnp.zeros((ROWS, LANES), jnp.float32)] * vectors
                for k in range(vector_part):
                    a = a_ref[g * GROUP + k, rows, :]
                    for v in range(vectors):
                        total = jnp.sum(a * xs[v][k : k + 1, :], axis=1, keepdims=True)
                        accs[v] = jnp.where(cycle == k, total, accs[v])
                full = dst[rows, :]
                for v in range(vectors):
                    if vectors == 1:
                        here = local // GROUP == g
                    else:
                        here = eighth == v * groups + g
                    full = jnp.where(here & (cycle < vector_part), accs[v], full)
                dst[rows, :] = full
            if vectors == 2:
                for c in range(unknowns // ROWS):
                    rows = slice(c * ROWS, (c + 1) * ROWS)
                    got = dot_ref[rows, :]
                    for k in range(1, MATRIX):
                        more = dot_ref[k * unknowns + c * ROWS : k * unknowns + (c + 1) * ROWS, :]
                        got = jnp.where(cycle == vector_part + k, more, got)
                    got = got + pltpu.roll(got, LANES // 2, 1)
                    here = (block < 2) & (local // GROUP == g) & (cycle >= vector_part)
                    dst[rows, :] = jnp.where(here, got, dst[rows, :])
            if x is not None:
                send(x, vectors, g, dst)

    halves()

    receive(0, keep(0))
    surface(uc, uk, near(0), lc, tk, 1.0)
    xr[...] = lc[...].T
    matvec(vc, 1, 1)
    receive(1, keep(1))
    lift(near(1), lc, tk)
    xr[...] = lc[...].T
    matvec(wc, 1, 2)

    def alpha(i):
        return time_step * sum(butcher[i])

    def coupling(i):
        return time_step * butcher[i][i] * dissipation * inv_weight

    def own(p, group):
        return p * own_sections + group % own_sections

    alphas = per_lane(lambda p, s: alpha(s))
    betas = per_lane(lambda p, s: alpha(s) * coupling(s))
    gc[...] = uc[...] + alphas * vc[...] + betas * wc[...]
    to_k_order(gc, uk)

    def add(face, value):
        near_ref[0, face] = near_ref[0, face] + alphas * near_ref[1, face] + betas * value

    volume(gc, uk, lc, tk, time_step)
    receive(2, add)
    surface(gc, uk, near(0), lc, tk, time_step)

    own_alphas = per_lane(lambda p, g: alpha(own(p, g)))
    own_betas = per_lane(lambda p, g: alpha(own(p, g)) * coupling(own(p, g)))
    own_couplings = per_lane(lambda p, g: coupling(own(p, g)))
    step = own_alphas * vc[...] + own_betas * wc[...]
    tend = lc[...]
    total = -step
    for shift in range(SECTIONS):
        moved = tend if shift == 0 else pltpu.roll(tend, shift * count, 1)
        weights = per_lane(lambda p, g: butcher[own(p, g)][(g - shift) % SECTIONS])
        total = total + weights * moved
    gc[...] = step
    operand(total)
    matvec(fc, own_sections, 3)
    receive(3, keep(0))
    for s in range(1, own_sections):
        def merge(face, value, s=s):
            near_ref[0, face] = jnp.where(block == s, value, near_ref[0, face])
        receive(3 + s, merge)
    lift(near(0), lc, tk)
    operand(own_couplings * lc[...])
    matvec(wc, own_sections)
    rows = (gc[...] + fc[...] + wc[...]).T
    for s in range(own_sections):
        out_ref[s] = rows[s * count : (s + 1) * count]
    for x in range(3 + own_sections):
        for which in range(4):
            copy(x, which).wait_send()


def on_device(u_start, inverses, neighbours, partners):
    count, unknowns = u_start.shape
    devices = lax.axis_size("elem")
    own_sections = SECTIONS // lax.axis_size("section")
    listed = partners.reshape(-1, LANES)
    exchanges = 3 + own_sections
    column = pltpu.VMEM((unknowns, LANES), jnp.float32)
    vmem = pl.BlockSpec(memory_space=pltpu.VMEM)
    change = pl.pallas_call(
        functools.partial(kernel, devices, count),
        out_shape=jax.ShapeDtypeStruct((own_sections, count, unknowns), jnp.float32),
        in_specs=[pl.BlockSpec(memory_space=pl.ANY)] * 4,
        out_specs=vmem,
        scratch_shapes=[
            pltpu.VMEM(u_start.shape, jnp.float32),
            pltpu.VMEM(neighbours.shape[::-1], jnp.int32),
            pltpu.VMEM(listed.shape, jnp.int32),
            pltpu.VMEM((count, unknowns, unknowns), jnp.float32),
            pltpu.VMEM((exchanges, 3 * count, unknowns), jnp.float32),
            pltpu.VMEM((exchanges, 2 * count, LANES), jnp.float32),
            pltpu.VMEM((exchanges, count, LANES), jnp.float32),
            pltpu.VMEM((6, LANES, LANES), jnp.bfloat16),
            pltpu.VMEM((2, 6, FIELDS * FACE, LANES), jnp.float32),
        ]
        + [column] * 10
        + [
            pltpu.VMEM((LANES, unknowns), jnp.float32),
            pltpu.VMEM((LANES, LANES), jnp.float32),
            pltpu.VMEM((count // GROUP, MATRIX * unknowns, 2 * unknowns), jnp.bfloat16),
            pltpu.VMEM((2 * unknowns, LANES), jnp.bfloat16),
            pltpu.VMEM((MATRIX * unknowns, LANES), jnp.float32),
            pltpu.VMEM((LANES, unknowns), jnp.float32),
            pltpu.SemaphoreType.DMA((3,)),
            pltpu.SemaphoreType.DMA((count // GROUP,)),
            pltpu.SemaphoreType.DMA((exchanges, 4)),
            pltpu.SemaphoreType.DMA((exchanges, 4)),
        ],
        compiler_params=pltpu.CompilerParams(
            collective_id=0, has_side_effects=True, vmem_limit_bytes=67_043_328
        ),
    )(u_start, neighbours.T, listed, inverses)
    return u_start[None] + change


def solution(mesh):
    placed = (P("elem", None), P("elem", None, None), P("elem", None), P())
    return jax.shard_map(
        on_device, mesh=mesh, in_specs=placed, out_specs=P("section", "elem", None), check_vma=False
    )
```
